512 devices in a mesh: rows: 128 (over z, y, core), cols: 4 (over x).
Axes of the slice: x: 4, y: 8, z: 8, core: 2. Of those that a mesh axis runs over, the one named last changes fastest.
Arguments:
- hidden_panel: float32 [8192, 16384], P('cols', 'rows'), may hold values from -6 to 6
- row_signs: float32 [16384], P('rows'), may hold values from -1 to 1, as said below
- sample_rows: int32 [128, 4], P('rows'), may hold values from 0 to 16383, as said below
- sample_counts: int32 [128], replicated, may hold values from 1 to 4, as said below
- ridge_weight: float32 [], replicated, may hold values from 0.5 to 2
Outputs:
- sketch_gram: float32 [8192, 8192], P('cols', 'rows')
The draws below stay inside these ranges and needn't reach their ends.
Inputs may be any that keep to these rules, and one draw needn't show every extreme that they name: `sample_rows`: row p holds 4 distinct row numbers of p * 128 to (p + 1) * 128 - 1 in ascending order, so the whole array ascends; only the first sample_counts[p] of them are sampled, the rest are ignored. `sample_counts`: entry p counts the live slots of block p; some block has exactly 4. `row_signs`: every entry is +1 or -1.
All inputs are finite; a program needn't handle non-finite values.
Results may differ from the reference program's by a relative error of at most 0.00008.
Values sent between devices are 32-bit elements; how exact they have to be, the bound alone decides.
A program may use at most 64 MiB of HBM per device.

```python
import math
import jax
import jax.numpy as jnp
from jax import lax

C = 8192
R_DEV = 128
MOST = 4
ROWS = 16384
N_ROWS = 128


def sample_plan(key):
    base_key = jax.random.fold_in(key, 11)
    count_key, top_key, pick_key = jax.random.split(base_key, 3)
    counts_drawn = jax.random.randint(count_key, (N_ROWS,), 1, MOST + 1)
    top_block = jax.random.randint(top_key, (), 0, N_ROWS)
    counts_drawn = jnp.where(jnp.arange(N_ROWS) == top_block, MOST, counts_drawn).astype(jnp.int32)
    block_keys = jax.random.split(pick_key, N_ROWS)

    def pick_block(block_key):
        return jnp.sort(jax.random.permutation(block_key, R_DEV)[:MOST])
    picks = jax.vmap(pick_block)(block_keys).astype(jnp.int32)
    rows_drawn = picks + jnp.arange(N_ROWS, dtype=jnp.int32)[:, None] * R_DEV
    return (rows_drawn.astype(jnp.int32), counts_drawn)


def draw_sample_rows(key, part):
    return sample_plan(key)[0]


def draw_sample_counts(key, part):
    return sample_plan(key)[1]


def draw_row_signs(key, part):
    coins = jax.random.randint(jax.random.fold_in(key, 5), (R_DEV * N_ROWS,), 0, 2)
    return (1 - 2 * coins).astype(jnp.float32)


def block_levels(stream_key, dims, cuts, smallest, high):
    factor_of = 1.0
    for position, shards_of in cuts:
        steps = jax.random.uniform(jax.random.fold_in(jax.random.fold_in(stream_key, 6), position), (shards_of,), jnp.float32, smallest / len(cuts), high / len(cuts))
        factor_of = factor_of * jnp.repeat(jnp.exp(steps), dims[position] // shards_of).reshape((-1,) + (1,) * (len(dims) - 1 - position))
    return factor_of


def bell_draw(key, shape, scale, most, cuts=(), kind=jnp.bfloat16):
    result = jax.random.normal(key, shape, jnp.float32) * scale
    if len(cuts) > 0:
        result = block_levels(key, shape, cuts, -0.22, 0.18) * result
    return jnp.clip(result, min=-most, max=most).astype(kind)


def setup_inputs(seed: int = 0) -> dict:
    seeds = jax.random.split(jax.random.key(seed), 6)
    return {
        "hidden_panel": bell_draw(seeds[0], (C, ROWS), 1.0, 6.0, ((0, 4), (1, 128)), jnp.float32),
        "row_signs": draw_row_signs(jax.random.fold_in(seeds[5], 71), 0),
        "sample_rows": draw_sample_rows(jax.random.fold_in(seeds[5], 71), 0),
        "sample_counts": draw_sample_counts(jax.random.fold_in(seeds[5], 71), 0),
        "ridge_weight": jnp.clip(jax.random.uniform(seeds[4], (), jnp.float32, 0.5, 2.0), 0.5, 2.0),
    }


def sign_table(extent):
    positions = jnp.arange(extent, dtype=jnp.int32)
    common = positions[:, None] & positions[None, :]
    parity = jnp.zeros_like(common)
    for bit_level in range(extent.bit_length() - 1):
        parity = parity ^ common >> bit_level & 1
    return (1 - 2 * parity).astype(jnp.float32)

def local_transform(signed):
    width, length = signed.shape
    outer_size = min(128, length)
    inner_size = length // outer_size
    blocks = signed.reshape(width, outer_size, inner_size)
    blocks = jnp.einsum('cab,ea->ceb', blocks, sign_table(outer_size), precision=lax.Precision.HIGHEST)
    blocks = jnp.einsum('ceb,fb->cef', blocks, sign_table(inner_size), precision=lax.Precision.HIGHEST)
    return blocks.reshape(width, length)

def reference(hidden_panel, row_signs, sample_rows, sample_counts, ridge_weight):
    columns_all, length_all = hidden_panel.shape
    shards = N_ROWS
    length = R_DEV
    block_cols = min(16, columns_all)
    flat_rows = sample_rows.reshape(-1).astype(jnp.int32)
    owner_shard = (flat_rows // length).astype(jnp.int32)
    local_rows = (flat_rows - owner_shard * length).astype(jnp.int32)
    weights_rows = sign_table(shards)[owner_shard]
    factor = 1.0 / math.sqrt(length * shards)

    def column_block(block):
        signed = block * row_signs[None, :]
        spread = local_transform(signed.reshape(block_cols * shards, length)).reshape(block_cols, shards, length)
        chosen = spread[:, :, local_rows]
        return jnp.einsum('cpk,kp->ck', chosen, weights_rows, precision=lax.Precision.HIGHEST) * factor
    sketch = lax.map(column_block, hidden_panel.reshape(columns_all // block_cols, block_cols, length_all))
    sketch = sketch.reshape(columns_all, -1)
    slot_mask = (jnp.arange(sample_rows.shape[1])[None, :] < sample_counts[:, None]).reshape(-1).astype(jnp.float32)
    sketch = sketch * slot_mask[None, :]
    gram = jnp.dot(sketch, sketch.T, precision=lax.Precision.HIGHEST, preferred_element_type=jnp.float32)
    sample_total = jnp.sum(sample_counts).astype(jnp.float32)
    return gram / sample_total + ridge_weight * jnp.eye(columns_all, dtype=jnp.float32)
```

```python
import functools
import math

import jax
import jax.numpy as jnp
from jax import lax
from jax.experimental import pallas as pl
from jax.experimental.pallas import tpu as pltpu
from jax.sharding import PartitionSpec as P

MESH = pl.DeviceIdType.MESH


def halves(value):
    high = value.astype(jnp.bfloat16)
    return high, (value - high.astype(jnp.float32)).astype(jnp.bfloat16)


def signs_of(common):
    for shift in (8, 4, 2, 1):
        common = common ^ (common >> shift)
    return (1 - 2 * (common & 1)).astype(jnp.float32)


def far_first(n):
    return [n // 2] + [d for k in range(n // 2 - 1, 0, -1) for d in (k, n - k)]


def kernel(
    nz, ny, nx, cap, panel, signs, rows, counts, ridge, out,
    xs, ra, rb, sm1, sm2, pa, pb, qa, qb, sa, sb, bo, b2, hh, ob, st,
    in_sem, out_sem, s_raw, r_raw, s_sm1, r_sm1, s_sm2, r_sm2, s_red, r_red, s_ag, r_ag,
    s_op, r_op, s_x, r_x, s_sib, r_sib, s_ring, r_ring, s_out, r_out,
):
    length = panel.shape[-1]
    shards = counts.shape[1]
    me = lax.axis_index("rows")
    q = lax.axis_index("cols")
    c = lax.rem(me, 2)
    y = lax.rem(me // 2, ny)
    z = me // (2 * ny)
    mate = 1 - c

    def at(zz, yy, cc, xx):
        return ((zz * ny + yy) * 2 + cc, xx)

    def up_z(d):
        return lax.rem(z + d, nz)

    def up_y(d):
        return lax.rem(y + d, ny)

    pending = []

    def send(src, dst, ss, rs, to, keep=True):
        copy = pltpu.make_async_remote_copy(
            src_ref=src, dst_ref=dst, send_sem=ss, recv_sem=rs, device_id=to, device_id_type=MESH
        )
        copy.start()
        if keep:
            pending.append(copy)
        return copy

    def arrived(slot, sem):
        pltpu.make_async_copy(slot, slot, sem).wait()

    load = pltpu.make_async_copy(panel, xs, in_sem)
    load.start()

    barrier = pltpu.get_barrier_semaphore()
    greeted = [at(z, y, mate, q)]
    for d in range(1, nz):
        greeted += [at(up_z(d), y, cc, q) for cc in (0, 1)]
    for d in range(1, ny):
        greeted += [at(z, up_y(d), cc, q) for cc in (0, 1)]
    for d in range(1, nx):
        greeted.append(at(z, y, c, lax.rem(q + d, nx)))
    for to in greeted:
        pl.semaphore_signal(barrier, inc=1, device_id=to, device_id_type=MESH)

    count_row = counts[...].astype(jnp.float32)
    lane = lax.broadcasted_iota(jnp.int32, (shards, shards), 1)
    line = lax.broadcasted_iota(jnp.int32, (shards, shards), 0)
    ends = jnp.sum(jnp.where(lane <= line, count_row, 0.0), axis=1, keepdims=True)
    slot = lax.broadcasted_iota(jnp.int32, (1, cap), 1)
    passed = ends <= slot.astype(jnp.float32)
    pk = jnp.sum(passed.astype(jnp.float32), axis=0, keepdims=True).astype(jnp.int32)
    block = lax.broadcasted_iota(jnp.int32, (1, shards), 1)
    before = jnp.sum(jnp.where(block < me, count_row, 0.0), axis=1, keepdims=True)
    total = jnp.sum(count_row, axis=1, keepdims=True)
    place = slot - before.astype(jnp.int32)
    own = jnp.zeros((1, cap), jnp.int32)
    for j in range(rows.shape[1]):
        own = jnp.where((pk == me) & (place == j), rows[0, j] - me * length, own)
    sm1[z, c] = own

    load.wait()
    xs[...] = xs[...] * signs[...]
    pl.semaphore_wait(barrier, len(greeted))

    send(sm1.at[z, c], sm1.at[z, c], s_sm1.at[0, 0], r_sm1.at[0, c], at(z, y, mate, q))
    for d in range(1, nz):
        for cc in (0, 1):
            send(sm1.at[z, c], sm1.at[z, c], s_sm1.at[d, cc], r_sm1.at[d, c], at(up_z(d), y, cc, q))

    def raw_z(d):
        for cc in (0, 1):
            send(xs.at[cc, :, 0, up_z(d)], ra.at[z, c], s_raw.at[0, d, cc], r_raw.at[0, d, c], at(up_z(d), y, cc, q))

    def raw_y(d):
        for cc in (0, 1):
            send(xs.at[cc, up_y(d), 1], rb.at[y, c], s_raw.at[1, d, cc], r_raw.at[1, d, c], at(z, up_y(d), cc, q))

    order_z, order_y = far_first(nz), far_first(ny)
    split = min(3, len(order_y))
    for k in range(max(len(order_z), split)):
        if k < len(order_z):
            raw_z(order_z[k])
        if k < split:
            raw_y(order_y[k])
    send(xs.at[mate, :, 0, z], ra.at[z, c], s_raw.at[0, 0, 0], r_raw.at[0, 0, c], at(z, y, mate, q))
    send(xs.at[mate, y, 1], rb.at[y, c], s_raw.at[1, 0, 0], r_raw.at[1, 0, c], at(z, y, mate, q))

    arrived(sm1.at[z, mate], r_sm1.at[0, mate])
    for d in range(1, nz):
        for cc in (0, 1):
            arrived(sm1.at[up_z(nz - d), cc], r_sm1.at[d, cc])
    sm2[y] = jnp.sum(sm1[...].reshape(2 * nz, 1, cap), axis=0)
    for d in range(1, ny):
        send(sm2.at[y], sm2.at[y], s_sm2.at[d], r_sm2.at[d], at(z, up_y(d), c, q))
    for d in order_y[split:]:
        raw_y(d)
    for d in range(1, ny):
        arrived(sm2.at[up_y(ny - d)], r_sm2.at[d])
    local_row = jnp.sum(sm2[...], axis=0)

    token = lax.broadcasted_iota(jnp.int32, (length, cap), 0)
    scale = 1.0 / math.sqrt(length * shards)
    live = jnp.where(slot.astype(jnp.float32) < total, scale, 0.0)
    sign = (signs_of(token & local_row) * live).astype(jnp.bfloat16)
    hh[:length] = sign
    hh[length:] = sign

    def share(parts, acc):
        pieces = [jnp.concatenate(halves(value), axis=1) for value, _ in parts]
        made = jnp.dot(jnp.concatenate(pieces, axis=0), hh[...], preferred_element_type=jnp.float32)
        high = made.shape[0] // len(parts)
        for k, (_, source) in enumerate(parts):
            term = made[k * high : (k + 1) * high] * signs_of(pk & source)
            acc = term if acc is None else acc + term
        return acc

    def batches(n):
        return [(0,)] + [(d, n - d) for d in range(1, n // 2)] + [(n // 2,)]

    def flat(value):
        return value.reshape(-1, value.shape[-1])

    def block_of(zz, yy, cc):
        return (zz * ny + yy) * 2 + cc

    def share_z():
        acc = None
        for batch in batches(nz):
            parts = []
            for d in batch:
                zz = up_z(nz - d) if d else z
                for cc in (0, 1):
                    if d == 0 and cc == 0:
                        parts.append((flat(xs[c, :, 0, z]), block_of(z, y, c)))
                        continue
                    source = mate if d == 0 else cc
                    arrived(ra.at[zz, source], r_raw.at[0, d, source])
                    parts.append((flat(ra[zz, source]), block_of(zz, y, source)))
            acc = share(parts, acc)
        return acc

    def share_y():
        acc = None
        for batch in batches(ny):
            parts = []
            for d in batch:
                yy = up_y(ny - d) if d else y
                for cc in (0, 1):
                    if d == 0 and cc == 0:
                        parts.append((flat(xs[c, y, 1]), block_of(z, y, c)))
                        continue
                    source = mate if d == 0 else cc
                    arrived(rb.at[yy, source], r_raw.at[1, d, source])
                    parts.append((flat(rb[yy, source]), block_of(z, yy, source)))
            acc = share(parts, acc)
        return acc

    pa[...] = share_z().reshape(ny, 8, cap)
    for d in far_first(ny):
        send(pa.at[up_y(d)], qa.at[y], s_red.at[0, d], r_red.at[0, d], at(z, up_y(d), c, q))
    pb[...] = share_y().reshape(nz, 8, cap)
    for d in far_first(nz):
        send(pb.at[up_z(d)], qb.at[z], s_red.at[1, d], r_red.at[1, d], at(up_z(d), y, c, q))

    piece = pa[y]
    for d in range(1, ny):
        arrived(qa.at[up_y(ny - d)], r_red.at[0, d])
        piece = piece + qa[up_y(ny - d)]
    sa[y, z] = piece
    for d in far_first(nz):
        send(sa.at[y, z], sa.at[y, z], s_ag.at[0, d], r_ag.at[0, d], at(up_z(d), y, c, q))
    piece = pb[z]
    for d in range(1, nz):
        arrived(qb.at[up_z(nz - d)], r_red.at[1, d])
        piece = piece + qb[up_z(nz - d)]
    sb[z, y] = piece
    for d in far_first(ny):
        send(sb.at[z, y], sb.at[z, y], s_ag.at[1, d], r_ag.at[1, d], at(z, up_y(d), c, q))

    target = 2 * q + c
    hop = lax.rem(target - z + nz, nz)

    @pl.when(hop != 0)
    def _():
        send(sb.at[z, y], bo.at[1, z], s_op.at[hop], r_op.at[hop], at(target, y, c, q), keep=False)

    @pl.when(hop == 0)
    def _():
        bo[1, z] = piece

    for d in range(1, nz):
        arrived(sa.at[y, up_z(nz - d)], r_ag.at[0, d])

    def ring(which, sign_of, d):
        n, mine, buf = (ny, y, sa) if which == 0 else (nz, z, sb)
        chunk = lax.rem(mine + n - d, n) if sign_of == 0 else lax.rem(mine + d, n)
        step = 1 if sign_of == 0 else n - 1
        there = lax.rem(mine + step, n)
        to = at(z, there, c, q) if which == 0 else at(there, y, c, q)
        view = buf.at[chunk]
        if d == n // 2 - 1:
            half = buf.shape[1] // 2
            view = buf.at[chunk, pl.ds(0 if sign_of == 0 else half, half)]
        send(view, view, s_ring.at[which, sign_of, d], r_ring.at[which, sign_of, d], to)

    def ring_wait(which, sign_of, d):
        n, mine, buf = (ny, y, sa) if which == 0 else (nz, z, sb)
        chunk = lax.rem(mine + n - d, n) if sign_of == 0 else lax.rem(mine + d, n)
        view = buf.at[chunk]
        if d == n // 2:
            half = buf.shape[1] // 2
            view = buf.at[chunk, pl.ds(0 if sign_of == 0 else half, half)]
        arrived(view, r_ring.at[which, sign_of, d - 1])

    for way in (0, 1):
        ring(0, way, 0)
    for d in range(1, ny):
        arrived(sb.at[z, up_y(ny - d)], r_ag.at[1, d])
    for way in (0, 1):
        ring(1, way, 0)

    root_c = lax.rem(z, 2)
    root_q = z // 2

    @pl.when((c == root_c) & (q == root_q))
    def _():
        for d in range(1, nz):
            arrived(bo.at[1, up_z(nz - d)], r_op.at[d])
        bo[0] = sa[y]
        for h in (0, 1):
            src = sa.at[y] if h == 0 else bo.at[1]
            for d in range(1, nx):
                send(src, bo.at[h], s_x.at[h, d], r_x.at[h, d], at(z, y, c, lax.rem(q + d, nx)), keep=False)
            send(src, bo.at[h], s_sib.at[h], r_sib.at[h], at(z, y, mate, q), keep=False)

    def ring_step(d):
        for which, n in ((0, ny), (1, nz)):
            if d < n // 2:
                for way in (0, 1):
                    ring_wait(which, way, d)
                    ring(which, way, d)

    top = max(ny, nz) // 2
    for d in range(1, top - 1):
        ring_step(d)

    away = lax.rem(q - root_q + nx, nx)

    @pl.when((c == root_c) & (q != root_q))
    def _():
        for h in (0, 1):
            arrived(bo.at[h], r_x.at[h, away])
            send(bo.at[h], bo.at[h], s_sib.at[h], r_sib.at[h], at(z, y, mate, q), keep=False)

    if top > 1:
        ring_step(top - 1)

    @pl.when(c != root_c)
    def _():
        for h in (0, 1):
            arrived(bo.at[h], r_sib.at[h])

    wide = 2 * nz * 8
    half_wide = wide // 2
    b_high, b_low = halves(flat(bo[...].reshape(2 * nz, 8, cap)))
    b2[:wide] = b_high
    b2[wide:] = b_low
    units = 2 * ny * wide
    first = q * units + c * (ny * wide)
    col = (z * ny + y) * wide + lax.broadcasted_iota(jnp.int32, (1, wide), 1)
    inverse = 1.0 / total
    weight = ridge[0, 0]

    def gram(which, chunk):
        value = flat(sa[chunk] if which == 0 else sb[chunk])
        high = value.shape[0]
        both = jnp.concatenate(halves(value), axis=0)
        made = lax.dot_general(both, b2[...], (((1,), (1,)), ((), ())), preferred_element_type=jnp.float32)
        made = made[:high] + made[high:]
        made = made[:, :wide] + made[:, wide:]
        r = lax.broadcasted_iota(jnp.int32, (high, 1), 0)
        if which == 0:
            unit = first + chunk * wide + r
        else:
            unit = first + (r // 8) * wide + half_wide + chunk * 8 + lax.rem(r, 8)
        made = made * inverse + jnp.where(unit == col, weight, 0.0)
        left, right = made[:, :half_wide], made[:, half_wide:]
        mine = jnp.where(c == 0, left, right).reshape(-1, 8, half_wide)
        theirs = jnp.where(c == 0, right, left).reshape(-1, 8, half_wide)
        return mine, theirs

    def emit(which, d):
        n, mine_at = (ny, y) if which == 0 else (nz, z)
        chunk = lax.rem(mine_at + d, n)
        mine, theirs = gram(which, chunk)
        if which == 0:
            ob[c, chunk, 0] = mine
            st[chunk, 0] = theirs
            src, dst = st.at[chunk, 0], ob.at[c, chunk, 0]
        else:
            ob[c, :, 1, chunk] = mine
            st[:, 1, chunk] = theirs
            src, dst = st.at[:, 1, chunk], ob.at[c, :, 1, chunk]
        send(src, dst, s_out.at[which, d], r_out.at[which, d], at(z, y, mate, q))

    for d in range(nz):
        if d != nz // 2:
            emit(1, d)
    for d in range(ny):
        if d != ny // 2:
            emit(0, d)
    for which, n in ((0, ny), (1, nz)):
        for way in (0, 1):
            ring_wait(which, way, n // 2)
        emit(which, n // 2)

    mine_out = pltpu.make_async_copy(ob.at[c], out.at[c], out_sem.at[0])
    mine_out.start()
    for which, n in ((0, ny), (1, nz)):
        for d in range(n):
            chunk = lax.rem((y if which == 0 else z) + d, n)
            arrived(ob.at[mate, chunk, 0] if which == 0 else ob.at[mate, :, 1, chunk], r_out.at[which, d])
    mate_out = pltpu.make_async_copy(ob.at[mate], out.at[mate], out_sem.at[1])
    mate_out.start()

    for copy in pending:
        copy.wait_send()

    def sent(src, sem):
        pltpu.make_async_copy(src, src, sem).wait()

    @pl.when(hop != 0)
    def _():
        sent(sb.at[z, y], s_op.at[hop])

    @pl.when((c == root_c) & (q == root_q))
    def _():
        for h in (0, 1):
            for d in range(1, nx):
                sent(bo.at[h], s_x.at[h, d])

    @pl.when(c == root_c)
    def _():
        for h in (0, 1):
            sent(bo.at[h], s_sib.at[h])

    mine_out.wait()
    mate_out.wait()


def body(hidden_panel, row_signs, sample_rows, sample_counts, ridge_weight):
    nx = lax.axis_size("cols")
    nz = 2 * nx
    ny = lax.axis_size("rows") // (2 * nz)
    width, length = hidden_panel.shape
    shards = sample_counts.shape[0]
    cap = -(-shards * sample_rows.shape[1] // 128) * 128
    half_wide = 8 * nz
    dma, f32, i32, bf16 = pltpu.SemaphoreType.DMA, jnp.float32, jnp.int32, jnp.bfloat16
    m = max(nz, ny)
    vmem = pl.BlockSpec(memory_space=pltpu.VMEM)
    smem = pl.BlockSpec(memory_space=pltpu.SMEM)
    hbm = pl.BlockSpec(memory_space=pl.ANY)
    result = pl.pallas_call(
        functools.partial(kernel, nz, ny, nx, cap),
        out_shape=jax.ShapeDtypeStruct((2, ny, 2, nz, 8, half_wide), f32),
        in_specs=[hbm, vmem, smem, vmem, smem],
        out_specs=hbm,
        scratch_shapes=[
            pltpu.VMEM((2, ny, 2, nz, 8, length), f32),
            pltpu.VMEM((nz, 2, ny, 8, length), f32),
            pltpu.VMEM((ny, 2, nz, 8, length), f32),
            pltpu.VMEM((nz, 2, 1, cap), i32),
            pltpu.VMEM((ny, 1, cap), i32),
            pltpu.VMEM((ny, 8, cap), f32),
            pltpu.VMEM((nz, 8, cap), f32),
            pltpu.VMEM((ny, 8, cap), f32),
            pltpu.VMEM((nz, 8, cap), f32),
            pltpu.VMEM((ny, nz, 8, cap), f32),
            pltpu.VMEM((nz, ny, 8, cap), f32),
            pltpu.VMEM((2, nz, 8, cap), f32),
            pltpu.VMEM((4 * half_wide, cap), bf16),
            pltpu.VMEM((2 * length, cap), bf16),
            pltpu.VMEM((2, ny, 2, nz, 8, half_wide), f32),
            pltpu.VMEM((ny, 2, nz, 8, half_wide), f32),
            dma(()),
            dma((2,)),
            dma((2, m, 2)),
            dma((2, m, 2)),
            dma((nz, 2)),
            dma((nz, 2)),
            dma((ny,)),
            dma((ny,)),
            dma((2, m)),
            dma((2, m)),
            dma((2, m)),
            dma((2, m)),
            dma((nz,)),
            dma((nz,)),
            dma((2, nx)),
            dma((2, nx)),
            dma((2,)),
            dma((2,)),
            dma((2, 2, m // 2)),
            dma((2, 2, m // 2)),
            dma((2, m)),
            dma((2, m)),
        ],
        compiler_params=pltpu.CompilerParams(collective_id=0, has_side_effects=True),
        name="sketch_gram",
    )(
        hidden_panel.reshape(2, ny, 2, nz, 8, length),
        row_signs.reshape(1, length),
        sample_rows,
        sample_counts.reshape(1, shards),
        ridge_weight.reshape(1, 1),
    )
    return result.reshape(width, half_wide)


def solution(mesh):
    placed = (P("cols", "rows"), P("rows"), P("rows", None), P(), P())
    return jax.shard_map(
        body, mesh=mesh, in_specs=placed, out_specs=P("cols", "rows"), check_vma=False
    )
```

```python
import functools
import math

import jax
import jax.numpy as jnp
from jax import lax
from jax.experimental import pallas as pl
from jax.experimental.pallas import tpu as pltpu
from jax.sharding import PartitionSpec as P

MESH = pl.DeviceIdType.MESH


def halves(value):
    high = value.astype(jnp.bfloat16)
    return high, (value - high.astype(jnp.float32)).astype(jnp.bfloat16)


def signs_of(common):
    for shift in (8, 4, 2, 1):
        common = common ^ (common >> shift)
    return (1 - 2 * (common & 1)).astype(jnp.float32)


def far_first(n):
    return [n // 2] + [d for k in range(n // 2 - 1, 0, -1) for d in (k, n - k)]


def near_first(n):
    return [d for k in range(1, n // 2) for d in (k, n - k)] + [n // 2]


SUBS = 4
GROUP = 4
PLAN = (((1, 3), "relay0"), ((2, 1), "relay1"), ((2, 3), "far0"), ((3, 0), "far1"), ((3, 2), "ready"))


def kernel(
    nz, ny, nx, cap, panel, signs, rows, counts, ridge, out,
    xs, ra, rb, sm1, sm2, pa, pb, qa, qb, sa, sb, bo, b2, hh, ob, st,
    in_sem, out_sem, s_raw, r_raw, s_sm1, r_sm1, s_sm2, r_sm2, s_red, r_red, s_ag, r_ag,
    s_op, r_op, s_x, r_x, s_sib, r_sib, s_ring, r_ring, s_out, r_out,
):
    length = panel.shape[-1]
    shards = counts.shape[1]
    me = lax.axis_index("rows")
    q = lax.axis_index("cols")
    c = lax.rem(me, 2)
    y = lax.rem(me // 2, ny)
    z = me // (2 * ny)
    mate = 1 - c

    def at(zz, yy, cc, xx):
        return ((zz * ny + yy) * 2 + cc, xx)

    def up_z(d):
        return lax.rem(z + d, nz)

    def up_y(d):
        return lax.rem(y + d, ny)

    pending = []

    def send(src, dst, ss, rs, to, keep=True):
        copy = pltpu.make_async_remote_copy(
            src_ref=src, dst_ref=dst, send_sem=ss, recv_sem=rs, device_id=to, device_id_type=MESH
        )
        copy.start()
        if keep:
            pending.append(copy)
        return copy

    def arrived(slot, sem):
        pltpu.make_async_copy(slot, slot, sem).wait()

    def sent(src, sem):
        pltpu.make_async_copy(src, src, sem).wait()

    load = pltpu.make_async_copy(panel, xs, in_sem)
    load.start()

    barrier = pltpu.get_barrier_semaphore()
    greeted = [at(z, y, mate, q)]
    for d in range(1, nz):
        greeted += [at(up_z(d), y, cc, q) for cc in (0, 1)]
    for d in range(1, ny):
        greeted += [at(z, up_y(d), cc, q) for cc in (0, 1)]
    for d in range(1, nx):
        greeted.append(at(z, y, c, lax.rem(q + d, nx)))
    for to in greeted:
        pl.semaphore_signal(barrier, inc=1, device_id=to, device_id_type=MESH)

    count_row = counts[...].astype(jnp.float32)
    lane = lax.broadcasted_iota(jnp.int32, (shards, shards), 1)
    line = lax.broadcasted_iota(jnp.int32, (shards, shards), 0)
    ends = jnp.sum(jnp.where(lane <= line, count_row, 0.0), axis=1, keepdims=True)
    slot = lax.broadcasted_iota(jnp.int32, (1, cap), 1)
    passed = ends <= slot.astype(jnp.float32)
    pk = jnp.sum(passed.astype(jnp.float32), axis=0, keepdims=True).astype(jnp.int32)
    block = lax.broadcasted_iota(jnp.int32, (1, shards), 1)
    before = jnp.sum(jnp.where(block < me, count_row, 0.0), axis=1, keepdims=True)
    total = jnp.sum(count_row, axis=1, keepdims=True)
    place = slot - before.astype(jnp.int32)
    own = jnp.zeros((1, cap), jnp.int32)
    for j in range(rows.shape[1]):
        own = jnp.where((pk == me) & (place == j), rows[0, j] - me * length, own)
    sm1[z, c] = own

    load.wait()
    xs[...] = xs[...] * signs[...]
    pl.semaphore_wait(barrier, len(greeted))

    @pl.when(c == 0)
    def _():
        send(sm1.at[z, 0], sm1.at[z, 0], s_sm1.at[0], r_sm1.at[0, 0], at(z, y, 1, q), keep=False)

    for d in range(1, nz):
        send(sm1.at[z, c], sm1.at[z, c], s_sm1.at[d], r_sm1.at[d, c], at(up_z(d), y, 1, q))

    def raw_z(d):
        for cc in (0, 1):
            send(xs.at[cc, :, 0, up_z(d)], ra.at[z, c], s_raw.at[0, d, cc], r_raw.at[0, d, c], at(up_z(d), y, cc, q), keep=False)

    def raw_y(d):
        for cc in (0, 1):
            send(xs.at[cc, up_y(d), 1], rb.at[y, c], s_raw.at[1, d, cc], r_raw.at[1, d, c], at(z, up_y(d), cc, q), keep=False)

    order_z, order_y = near_first(nz), near_first(ny)

    @pl.when(c == 0)
    def _():
        for k in range(max(len(order_z), len(order_y))):
            if k < len(order_z):
                raw_z(order_z[k])
            if k < len(order_y):
                raw_y(order_y[k])

    @pl.when(c == 1)
    def _():
        for d in order_z:
            raw_z(d)
        arrived(sm1.at[z, 0], r_sm1.at[0, 0])
        for d in range(1, nz):
            for cc in (0, 1):
                arrived(sm1.at[up_z(nz - d), cc], r_sm1.at[d, cc])
        sm2[y] = jnp.sum(sm1[...].reshape(2 * nz, 1, cap), axis=0)
        for d in range(1, ny):
            for cc in (0, 1):
                send(sm2.at[y], sm2.at[y], s_sm2.at[d, cc], r_sm2.at[d], at(z, up_y(d), cc, q), keep=False)
        send(sm2.at[y], sm2.at[y], s_sm2.at[0, 0], r_sm2.at[0], at(z, y, 0, q), keep=False)
        for d in order_y:
            raw_y(d)

    send(xs.at[mate, :, 0, z], ra.at[z, c], s_raw.at[0, 0, 0], r_raw.at[0, 0, c], at(z, y, mate, q))
    send(xs.at[mate, y, 1], rb.at[y, c], s_raw.at[1, 0, 0], r_raw.at[1, 0, c], at(z, y, mate, q))

    @pl.when(c == 0)
    def _():
        arrived(sm2.at[y], r_sm2.at[0])

    for d in range(1, ny):
        arrived(sm2.at[up_y(ny - d)], r_sm2.at[d])
    local_row = jnp.sum(sm2[...], axis=0)

    token = lax.broadcasted_iota(jnp.int32, (length, cap), 0)
    scale = 1.0 / math.sqrt(length * shards)
    live = jnp.where(slot.astype(jnp.float32) < total, scale, 0.0)
    sign = (signs_of(token & local_row) * live).astype(jnp.bfloat16)
    hh[:length] = sign
    hh[length:] = sign

    def share(parts, acc):
        pieces = [jnp.concatenate(halves(value), axis=1) for value, _ in parts]
        made = jnp.dot(jnp.concatenate(pieces, axis=0), hh[...], preferred_element_type=jnp.float32)
        high = made.shape[0] // len(parts)
        for k, (_, source) in enumerate(parts):
            term = made[k * high : (k + 1) * high] * signs_of(pk & source)
            acc = term if acc is None else acc + term
        return acc

    def batches(n):
        return [(0,)] + [(d, n - d) for d in range(1, n // 2)] + [(n // 2,)]

    def flat(value):
        return value.reshape(-1, value.shape[-1])

    def block_of(zz, yy, cc):
        return (zz * ny + yy) * 2 + cc

    def share_of(which, batch, acc):
        n, mine, buf = (nz, z, ra) if which == 0 else (ny, y, rb)
        parts = []
        for d in batch:
            far = lax.rem(mine + n - d, n) if d else mine
            for cc in (0, 1):
                if d == 0 and cc == 0:
                    held = xs[c, :, 0, z] if which == 0 else xs[c, y, 1]
                    parts.append((flat(held), block_of(z, y, c)))
                    continue
                source = mate if d == 0 else cc
                arrived(buf.at[far, source], r_raw.at[which, d, source])
                block_at = block_of(far, y, source) if which == 0 else block_of(z, far, source)
                parts.append((flat(buf[far, source]), block_at))
        return share(parts, acc)

    steps_z, steps_y = batches(nz), batches(ny)
    acc_z = acc_y = None
    for k in range(max(len(steps_z), len(steps_y))):
        if k < len(steps_z):
            acc_z = share_of(0, steps_z[k], acc_z)
            if k == len(steps_z) - 1:
                pa[...] = acc_z.reshape(ny, 8, cap)
                for d in far_first(ny):
                    send(pa.at[up_y(d)], qa.at[y], s_red.at[0, d], r_red.at[0, d], at(z, up_y(d), c, q))
        if k < len(steps_y):
            acc_y = share_of(1, steps_y[k], acc_y)
            if k == len(steps_y) - 1:
                pb[...] = acc_y.reshape(nz, 8, cap)
                for d in far_first(nz):
                    send(pb.at[up_z(d)], qb.at[z], s_red.at[1, d], r_red.at[1, d], at(up_z(d), y, c, q))

    subs = min(SUBS, nz, ny)

    def hold(which, d, k):
        n, mine, buf = (ny, y, sa) if which == 0 else (nz, z, sb)
        size = buf.shape[1] // subs
        return buf.at[lax.rem(mine + d, n), pl.ds(k * size, size)]

    extent = (ny, nz)

    def come_from(which, way, d):
        return (extent[which] - d) % extent[which] if way == 0 else d

    def passes(which, way, d, k):
        n = extent[which]
        return d < n // 2 or (d == n // 2 and k % 2 == way)

    def pass_on(which, d, k, ways=(0, 1)):
        n = extent[which]
        for way in ways:
            if not passes(which, way, d + 1, k):
                continue
            view = hold(which, come_from(which, way, d), k)
            step = 1 if way == 0 else n - 1
            to = at(z, up_y(step), c, q) if which == 0 else at(up_z(step), y, c, q)
            send(view, view, s_ring.at[which, way, d, k], r_ring.at[which, way, d, k], to)

    def take(which, d, k):
        for way in (0, 1):
            if passes(which, way, d, k):
                view = hold(which, come_from(which, way, d), k)
                arrived(view, r_ring.at[which, way, d - 1, k])
                pass_on(which, d, k, (way,))

    target = 2 * q + c
    hop = lax.rem(target - z + nz, nz)

    piece = pa[y]
    for d in range(1, ny):
        arrived(qa.at[up_y(ny - d)], r_red.at[0, d])
        piece = piece + qa[up_y(ny - d)]
    sa[y, z] = piece
    for d in far_first(nz):
        send(sa.at[y, z], sa.at[y, z], s_ag.at[0, d], r_ag.at[0, d], at(up_z(d), y, c, q))
    piece = pb[z]
    for d in range(1, nz):
        arrived(qb.at[up_z(nz - d)], r_red.at[1, d])
        piece = piece + qb[up_z(nz - d)]
    sb[z, y] = piece

    @pl.when(hop != 0)
    def _():
        send(sb.at[z, y], bo.at[1, z], s_op.at[hop], r_op.at[hop], at(target, y, c, q), keep=False)

    @pl.when(hop == 0)
    def _():
        bo[1, z] = piece

    for d in far_first(ny):
        send(sb.at[z, y], sb.at[z, y], s_ag.at[1, d], r_ag.at[1, d], at(z, up_y(d), c, q))
    for e in range(1, nz):
        arrived(sa.at[y, up_z(nz - e)], r_ag.at[0, e])
    for k in range(subs):
        pass_on(0, 0, k)
    for e in range(1, ny):
        arrived(sb.at[z, up_y(ny - e)], r_ag.at[1, e])
    for k in range(subs):
        pass_on(1, 0, k)

    root_c = lax.rem(z, 2)
    root_q = z // 2
    away = lax.rem(q - root_q + nx, nx)
    beside = [d for d in (1, nx - 1) if d] if nx > 2 else [1]
    mid = nz // 2

    @pl.when((c == root_c) & (away == 0))
    def _():
        for d in beside:
            send(sa.at[y], bo.at[0], s_x.at[0, d], r_x.at[0, 0], at(z, y, c, lax.rem(q + d, nx)), keep=False)
        send(sa.at[y], bo.at[0], s_sib.at[0], r_sib.at[0], at(z, y, mate, q), keep=False)
        for d in range(1, nz):
            arrived(bo.at[1, up_z(nz - d)], r_op.at[d])
        for d in beside:
            send(bo.at[1], bo.at[1], s_x.at[1, d], r_x.at[1, 0], at(z, y, c, lax.rem(q + d, nx)), keep=False)
        send(bo.at[1], bo.at[1], s_sib.at[1], r_sib.at[1], at(z, y, mate, q), keep=False)
        bo[0] = sa[y]

    def relay(h):
        for d in beside:
            part = pl.ds(0 if d == 1 else mid, mid)

            @pl.when((c == root_c) & (away == d))
            def _():
                arrived(bo.at[h], r_x.at[h, 0])
                if nx > 2:
                    there = lax.rem(root_q + 2, nx)
                    view = bo.at[h, part]
                    send(view, view, s_x.at[h, 2], r_x.at[h, d], at(z, y, c, there), keep=False)
                send(bo.at[h], bo.at[h], s_sib.at[h], r_sib.at[h], at(z, y, mate, q), keep=False)

    def relay_far(h):
        if nx > 2:

            @pl.when((c == root_c) & (away == 2))
            def _():
                for d in beside:
                    view = bo.at[h, pl.ds(0 if d == 1 else mid, mid)]
                    arrived(view, r_x.at[h, d])
                send(bo.at[h], bo.at[h], s_sib.at[h], r_sib.at[h], at(z, y, mate, q), keep=False)

    wide = 2 * nz * 8
    half_wide = wide // 2

    now_ready = [False]

    def columns_ready():
        @pl.when(c != root_c)
        def _():
            for h in (0, 1):
                arrived(bo.at[h], r_sib.at[h])

        b_high, b_low = halves(flat(bo[...].reshape(2 * nz, 8, cap)))
        b2[:, :wide] = b_high.T
        b2[:, wide:] = b_low.T

    def ready_now():
        columns_ready()
        now_ready[0] = True

    def tail_relays():
        for name in ("relay0", "relay1", "far0", "far1"):
            if name not in acted:
                act_of[name]()
        ready_now()

    acted = set()

    def once(name, act):
        def run():
            if name not in acted:
                acted.add(name)
                act()

        return run

    act_of = {
        "relay0": once("relay0", lambda: relay(0)),
        "relay1": once("relay1", lambda: relay(1)),
        "far0": once("far0", lambda: relay_far(0)),
        "far1": once("far1", lambda: relay_far(1)),
        "ready": once("ready", tail_relays),
    }

    units = 2 * ny * wide
    first = q * units + c * (ny * wide)
    col = (z * ny + y) * wide + lax.broadcasted_iota(jnp.int32, (1, wide), 1)
    inverse = 1.0 / total
    weight = ridge[0, 0]

    def emit(group):
        pieces, rows_of = [], []
        for which, d in group:
            n, mine = (ny, y) if which == 0 else (nz, z)
            chunk = lax.rem(mine + d, n)
            value = flat(sa[chunk] if which == 0 else sb[chunk])
            pieces += halves(value)
            r = lax.broadcasted_iota(jnp.int32, (value.shape[0], 1), 0)
            if which == 0:
                unit = first + chunk * wide + r
            else:
                unit = first + (r // 8) * wide + half_wide + chunk * 8 + lax.rem(r, 8)
            rows_of.append((which, chunk, unit))
        made = jnp.dot(jnp.concatenate(pieces, axis=0), b2[...], preferred_element_type=jnp.float32)
        made = made[:, :wide] + made[:, wide:]
        at_row = 0
        for which, chunk, unit in rows_of:
            high = unit.shape[0]
            part = made[at_row : at_row + high] + made[at_row + high : at_row + 2 * high]
            at_row += 2 * high
            part = (part * inverse + jnp.where(unit == col, weight, 0.0)).reshape(-1, 8, wide)
            if which == 0:
                ob[chunk, 0] = part
            else:
                ob[:, 1, chunk] = part

    work = [(1, 0), (0, 0)]
    for d in range(1, max(ny, nz) // 2):
        for which in (1, 0):
            if d < extent[which] // 2:
                work += [(which, d), (which, extent[which] - d)]

    top = max(ny, nz) // 2
    done = 0
    for d in range(1, top + 1):
        for k in range(subs):
            for which in (0, 1):
                if d <= extent[which] // 2:
                    take(which, d, k)
            for now, act in PLAN:
                if now == (d, k):
                    act_of[act]()
            able = [w for w in work[done:] if min(w[1], extent[w[0]] - w[1]) < d]
            if now_ready[0] and able:
                emit(able[:GROUP])
                done += len(able[:GROUP])
    if not now_ready[0]:
        act_of["ready"]()
    while done < len(work):
        emit(work[done : done + GROUP])
        done += GROUP
    emit([(which, extent[which] // 2) for which in (1, 0)])

    puts = []
    for k in range(ny):
        st[k] = ob[k].reshape(wide, wide).T.reshape(2, half_wide, wide)
        lanes = pl.ds(pl.multiple_of((c * ny + k) * wide, wide), wide)
        send(st.at[k, mate], out.at[:, lanes], s_out.at[k], r_out.at[k], at(z, y, mate, q))
        put = pltpu.make_async_copy(st.at[k, c], out.at[:, lanes], out_sem.at[k])
        put.start()
        puts.append(put)
    for k in range(ny):
        lanes = pl.ds(pl.multiple_of((mate * ny + k) * wide, wide), wide)
        arrived(out.at[:, lanes], r_out.at[k])
    for put in puts:
        put.wait()

    for copy in pending:
        copy.wait_send()
    for d in range(1, nz):
        for cc in (0, 1):
            sent(ra.at[0, 0], s_raw.at[0, d, cc])
    for d in range(1, ny):
        for cc in (0, 1):
            sent(rb.at[0, 0], s_raw.at[1, d, cc])

    @pl.when(c == 0)
    def _():
        sent(sm1.at[0, 0], s_sm1.at[0])

    @pl.when(c == 1)
    def _():
        for d in range(1, ny):
            for cc in (0, 1):
                sent(sm2.at[0], s_sm2.at[d, cc])
        sent(sm2.at[0], s_sm2.at[0, 0])

    @pl.when(hop != 0)
    def _():
        sent(sb.at[z, y], s_op.at[hop])

    @pl.when((c == root_c) & (away == 0))
    def _():
        for h in (0, 1):
            for d in beside:
                sent(bo.at[h], s_x.at[h, d])

    if nx > 2:

        @pl.when((c == root_c) & (lax.rem(away, 2) == 1))
        def _():
            for h in (0, 1):
                sent(bo.at[h, pl.ds(0, mid)], s_x.at[h, 2])

    @pl.when(c == root_c)
    def _():
        for h in (0, 1):
            sent(bo.at[h], s_sib.at[h])


def body(hidden_panel, row_signs, sample_rows, sample_counts, ridge_weight):
    nx = lax.axis_size("cols")
    nz = 2 * nx
    ny = lax.axis_size("rows") // (2 * nz)
    width, length = hidden_panel.shape
    shards = sample_counts.shape[0]
    cap = -(-shards * sample_rows.shape[1] // 128) * 128
    half_wide = 8 * nz
    dma, f32, i32, bf16 = pltpu.SemaphoreType.DMA, jnp.float32, jnp.int32, jnp.bfloat16
    m = max(nz, ny)
    vmem = pl.BlockSpec(memory_space=pltpu.VMEM)
    smem = pl.BlockSpec(memory_space=pltpu.SMEM)
    hbm = pl.BlockSpec(memory_space=pl.ANY)
    result = pl.pallas_call(
        functools.partial(kernel, nz, ny, nx, cap),
        out_shape=jax.ShapeDtypeStruct((half_wide, width), f32),
        in_specs=[hbm, vmem, smem, vmem, smem],
        out_specs=hbm,
        scratch_shapes=[
            pltpu.VMEM((2, ny, 2, nz, 8, length), f32),
            pltpu.VMEM((nz, 2, ny, 8, length), f32),
            pltpu.VMEM((ny, 2, nz, 8, length), f32),
            pltpu.VMEM((nz, 2, 1, cap), i32),
            pltpu.VMEM((ny, 1, cap), i32),
            pltpu.VMEM((ny, 8, cap), f32),
            pltpu.VMEM((nz, 8, cap), f32),
            pltpu.VMEM((ny, 8, cap), f32),
            pltpu.VMEM((nz, 8, cap), f32),
            pltpu.VMEM((ny, nz, 8, cap), f32),
            pltpu.VMEM((nz, ny, 8, cap), f32),
            pltpu.VMEM((2, nz, 8, cap), f32),
            pltpu.VMEM((cap, 4 * half_wide), bf16),
            pltpu.VMEM((2 * length, cap), bf16),
            pltpu.VMEM((ny, 2, nz, 8, 2 * half_wide), f32),
            pltpu.VMEM((ny, 2, half_wide, 2 * half_wide), f32),
            dma(()),
            dma((ny,)),
            dma((2, m, 2)),
            dma((2, m, 2)),
            dma((nz,)),
            dma((nz, 2)),
            dma((ny, 2)),
            dma((ny,)),
            dma((2, m)),
            dma((2, m)),
            dma((2, m)),
            dma((2, m)),
            dma((nz,)),
            dma((nz,)),
            dma((2, nx)),
            dma((2, nx)),
            dma((2,)),
            dma((2,)),
            dma((2, 2, m // 2, m)),
            dma((2, 2, m // 2, m)),
            dma((ny,)),
            dma((ny,)),
        ],
        compiler_params=pltpu.CompilerParams(collective_id=0, has_side_effects=True),
        name="sketch_gram",
    )(
        hidden_panel.reshape(2, ny, 2, nz, 8, length),
        row_signs.reshape(1, length),
        sample_rows,
        sample_counts.reshape(1, shards),
        ridge_weight.reshape(1, 1),
    )
    return result.T


def solution(mesh):
    placed = (P("cols", "rows"), P("rows"), P("rows", None), P(), P())
    return jax.shard_map(
        body, mesh=mesh, in_specs=placed, out_specs=P("cols", "rows"), check_vma=False
    )
```

```python
import functools
import math

import jax
import jax.numpy as jnp
from jax import lax
from jax.experimental import pallas as pl
from jax.experimental.pallas import tpu as pltpu
from jax.sharding import PartitionSpec as P

MESH = pl.DeviceIdType.MESH


def halves(value):
    high = value.astype(jnp.bfloat16)
    return high, (value - high.astype(jnp.float32)).astype(jnp.bfloat16)


def wrap(value, n):
    return value & (n - 1) if n & (n - 1) == 0 else lax.rem(value, n)


def signs_of(common):
    for shift in (8, 4, 2, 1):
        common = common ^ (common >> shift)
    return (1 - 2 * (common & 1)).astype(jnp.float32)


def far_first(n):
    return [n // 2] + [d for k in range(n // 2 - 1, 0, -1) for d in (k, n - k)]


def near_first(n):
    return [d for k in range(1, n // 2) for d in (k, n - k)] + [n // 2]


SUBS = 4
GROUP = 4
PLAN = (((1, 3), "relay0"), ((2, 1), "relay1"), ((2, 3), "far0"), ((3, 0), "far1"), ((3, 2), "ready"))


def kernel(
    nz, ny, nx, cap, panel, signs, rows, counts, ridge, out,
    xs, ra, rb, sm1, sm2, pa, pb, qa, qb, sa, sb, bo, bn, b2, hh, ob, st,
    in_sem, s_raw, r_raw, s_sm1, r_sm1, s_sm2, r_sm2, s_red, r_red, s_ag, r_ag,
    s_op, r_op, s_x, r_x, s_sib, r_sib, s_ring, r_ring, s_out, r_out,
):
    length = panel.shape[-1]
    shards = counts.shape[1]
    me = lax.axis_index("rows")
    q = lax.axis_index("cols")
    c = wrap(me, 2)
    y = wrap(me >> 1, ny)
    z = (me >> 1) // ny if ny & (ny - 1) else me >> ny.bit_length()
    mate = 1 - c

    def at(zz, yy, cc, xx):
        return ((zz * ny + yy) * 2 + cc, xx)

    def up_z(d):
        return wrap(z + d, nz)

    def up_y(d):
        return wrap(y + d, ny)

    pending = []

    def send(src, dst, ss, rs, to, keep=True):
        copy = pltpu.make_async_remote_copy(
            src_ref=src, dst_ref=dst, send_sem=ss, recv_sem=rs, device_id=to, device_id_type=MESH
        )
        copy.start()
        if keep:
            pending.append(copy)
        return copy

    def arrived(slot, sem):
        pltpu.make_async_copy(slot, slot, sem).wait()

    def sent(src, sem):
        pltpu.make_async_copy(src, src, sem).wait()

    load = pltpu.make_async_copy(panel, xs, in_sem)
    load.start()

    barrier = pltpu.get_barrier_semaphore()
    greeted = [at(z, y, mate, q)]
    for d in range(1, nz):
        greeted += [at(up_z(d), y, cc, q) for cc in (0, 1)]
    for d in range(1, ny):
        greeted += [at(z, up_y(d), cc, q) for cc in (0, 1)]
    for d in range(1, nx):
        greeted.append(at(z, y, c, wrap(q + d, nx)))
    for to in greeted:
        pl.semaphore_signal(barrier, inc=1, device_id=to, device_id_type=MESH)

    count_row = counts[...].astype(jnp.float32)
    lane = lax.broadcasted_iota(jnp.int32, (shards, shards), 1)
    line = lax.broadcasted_iota(jnp.int32, (shards, shards), 0)
    ends = jnp.sum(jnp.where(lane <= line, count_row, 0.0), axis=1, keepdims=True)
    slot = lax.broadcasted_iota(jnp.int32, (1, cap), 1)
    passed = ends <= slot.astype(jnp.float32)
    pk = jnp.sum(passed.astype(jnp.float32), axis=0, keepdims=True).astype(jnp.int32)
    block = lax.broadcasted_iota(jnp.int32, (1, shards), 1)
    before = jnp.sum(jnp.where(block < me, count_row, 0.0), axis=1, keepdims=True)
    total = jnp.sum(count_row, axis=1, keepdims=True)
    place = slot - before.astype(jnp.int32)
    own = jnp.zeros((1, cap), jnp.int32)
    for j in range(rows.shape[1]):
        own = jnp.where((pk == me) & (place == j), rows[0, j] - me * length, own)
    sm1[z, c] = own

    load.wait()
    xs[...] = xs[...] * signs[...]
    pl.semaphore_wait(barrier, len(greeted))

    @pl.when(c == 0)
    def _():
        send(sm1.at[z, 0], sm1.at[z, 0], s_sm1.at[0], r_sm1.at[0, 0], at(z, y, 1, q), keep=False)

    for d in range(1, nz):
        send(sm1.at[z, c], sm1.at[z, c], s_sm1.at[d], r_sm1.at[d, c], at(up_z(d), y, 1, q))

    def raw_z(d):
        for cc in (0, 1):
            send(xs.at[cc, :, 0, up_z(d)], ra.at[z, c], s_raw.at[0, d, cc], r_raw.at[0, d, c], at(up_z(d), y, cc, q), keep=False)

    def raw_y(d):
        for cc in (0, 1):
            send(xs.at[cc, up_y(d), 1], rb.at[y, c], s_raw.at[1, d, cc], r_raw.at[1, d, c], at(z, up_y(d), cc, q), keep=False)

    send(xs.at[mate, :, 0, z], ra.at[z, c], s_raw.at[0, 0, 0], r_raw.at[0, 0, c], at(z, y, mate, q))
    send(xs.at[mate, y, 1], rb.at[y, c], s_raw.at[1, 0, 0], r_raw.at[1, 0, c], at(z, y, mate, q))

    order_z, order_y = near_first(nz), near_first(ny)

    @pl.when(c == 0)
    def _():
        for k in range(max(len(order_z), len(order_y))):
            if k < len(order_z):
                raw_z(order_z[k])
            if k < len(order_y):
                raw_y(order_y[k])

    @pl.when(c == 1)
    def _():
        for d in order_z:
            raw_z(d)
        arrived(sm1.at[z, 0], r_sm1.at[0, 0])
        for d in range(1, nz):
            for cc in (0, 1):
                arrived(sm1.at[up_z(nz - d), cc], r_sm1.at[d, cc])
        sm2[y] = jnp.sum(sm1[...].reshape(2 * nz, 1, cap), axis=0)
        for d in range(1, ny):
            for cc in (0, 1):
                send(sm2.at[y], sm2.at[y], s_sm2.at[d, cc], r_sm2.at[d], at(z, up_y(d), cc, q), keep=False)
        send(sm2.at[y], sm2.at[y], s_sm2.at[0, 0], r_sm2.at[0], at(z, y, 0, q), keep=False)
        for d in order_y:
            raw_y(d)

    @pl.when(c == 0)
    def _():
        arrived(sm2.at[y], r_sm2.at[0])

    for d in range(1, ny):
        arrived(sm2.at[up_y(ny - d)], r_sm2.at[d])
    local_row = jnp.sum(sm2[...], axis=0)

    token = lax.broadcasted_iota(jnp.int32, (length, cap), 0)
    scale = 1.0 / math.sqrt(length * shards)
    live = jnp.where(slot.astype(jnp.float32) < total, scale, 0.0)
    sign = (signs_of(token & local_row) * live).astype(jnp.bfloat16)
    hh[:length] = sign
    hh[length:] = sign

    def share(parts, acc):
        pieces = [jnp.concatenate(halves(value), axis=1) for value, _ in parts]
        made = jnp.dot(jnp.concatenate(pieces, axis=0), hh[...], preferred_element_type=jnp.float32)
        high = made.shape[0] // len(parts)
        for k, (_, source) in enumerate(parts):
            term = made[k * high : (k + 1) * high] * signs_of(pk & source)
            acc = term if acc is None else acc + term
        return acc

    def batches(n):
        return [(0,)] + [(d, n - d) for d in range(1, n // 2)] + [(n // 2,)]

    def flat(value):
        return value.reshape(-1, value.shape[-1])

    def block_of(zz, yy, cc):
        return (zz * ny + yy) * 2 + cc

    def share_of(which, batch, acc):
        n, mine, buf = (nz, z, ra) if which == 0 else (ny, y, rb)
        parts = []
        for d in batch:
            far = wrap(mine + n - d, n) if d else mine
            for cc in (0, 1):
                if d == 0 and cc == 0:
                    held = xs[c, :, 0, z] if which == 0 else xs[c, y, 1]
                    parts.append((flat(held), block_of(z, y, c)))
                    continue
                source = mate if d == 0 else cc
                arrived(buf.at[far, source], r_raw.at[which, d, source])
                block_at = block_of(far, y, source) if which == 0 else block_of(z, far, source)
                parts.append((flat(buf[far, source]), block_at))
        return share(parts, acc)

    steps_z, steps_y = batches(nz), batches(ny)
    acc_z = acc_y = None
    for k in range(max(len(steps_z), len(steps_y))):
        if k < len(steps_z):
            acc_z = share_of(0, steps_z[k], acc_z)
            if k == len(steps_z) - 1:
                pa[...] = acc_z.reshape(ny, 8, cap)
                for d in far_first(ny):
                    send(pa.at[up_y(d)], qa.at[y], s_red.at[0, d], r_red.at[0, d], at(z, up_y(d), c, q))
        if k < len(steps_y):
            acc_y = share_of(1, steps_y[k], acc_y)
            if k == len(steps_y) - 1:
                pb[...] = acc_y.reshape(nz, 8, cap)
                for d in far_first(nz):
                    send(pb.at[up_z(d)], qb.at[z], s_red.at[1, d], r_red.at[1, d], at(up_z(d), y, c, q))

    subs = min(SUBS, nz, ny)

    def hold(which, d, k):
        n, mine, buf = (ny, y, sa) if which == 0 else (nz, z, sb)
        size = buf.shape[1] // subs
        return buf.at[wrap(mine + d, n), pl.ds(k * size, size)]

    extent = (ny, nz)
    orders = ([0] + near_first(nz), [0] + near_first(ny))

    def come_from(which, way, d):
        return (extent[which] - d) % extent[which] if way == 0 else d

    def passes(which, way, d, k):
        n = extent[which]
        return d < n // 2 or (d == n // 2 and k % 2 == way)

    def pass_on(which, d, k, ways=(0, 1)):
        n = extent[which]
        leap = min(2, n // 2)
        for way in ways:
            view = hold(which, come_from(which, way, d), k)
            for far in ([d + 1] if d + 1 < n // 2 else []) + ([n // 2] if d == n // 2 - leap else []):
                if not passes(which, way, far, k):
                    continue
                step = far - d if way == 0 else n - (far - d)
                to = at(z, up_y(step), c, q) if which == 0 else at(up_z(step), y, c, q)
                send(view, view, s_ring.at[which, way, far - 1, k], r_ring.at[which, way, far - 1, k], to)

    def take(which, d, k):
        for way in (0, 1):
            if passes(which, way, d, k):
                view = hold(which, come_from(which, way, d), k)
                arrived(view, r_ring.at[which, way, d - 1, k])
                pass_on(which, d, k, (way,))

    target = 2 * q + c
    hop = wrap(target - z + nz, nz)

    piece = pa[y]
    for d in range(1, ny):
        arrived(qa.at[up_y(ny - d)], r_red.at[0, d])
        piece = piece + qa[up_y(ny - d)]
    sa[y, 0] = piece
    for d in near_first(nz):
        send(sa.at[y, 0], sa.at[y, orders[0].index(d)], s_ag.at[0, d], r_ag.at[0, d], at(up_z(d), y, c, q))
    piece = pb[z]
    for d in range(1, nz):
        arrived(qb.at[up_z(nz - d)], r_red.at[1, d])
        piece = piece + qb[up_z(nz - d)]
    sb[z, 0] = piece

    @pl.when(hop != 0)
    def _():
        send(sb.at[z, 0], bo.at[1, z], s_op.at[hop], r_op.at[hop], at(target, y, c, q), keep=False)

    @pl.when(hop == 0)
    def _():
        bo[1, z] = piece

    for d in near_first(ny):
        send(sb.at[z, 0], sb.at[z, orders[1].index(d)], s_ag.at[1, d], r_ag.at[1, d], at(z, up_y(d), c, q))
    for k in range(subs):
        for which in (0, 1):
            mine, buf = (y, sa) if which == 0 else (z, sb)
            size = buf.shape[1] // subs
            for place_of in range(k * size, (k + 1) * size):
                e = orders[which][place_of]
                if e:
                    arrived(buf.at[mine, place_of], r_ag.at[which, e])
            pass_on(which, 0, k)

    root_c = wrap(z, 2)
    root_q = z >> 1
    away = wrap(q - root_q + nx, nx)
    beside = [d for d in (1, nx - 1) if d] if nx > 2 else [1]
    mid = nz // 2

    @pl.when((c == root_c) & (away == 0))
    def _():
        for d in beside:
            send(sa.at[y], bo.at[0], s_x.at[0, d], r_x.at[0, 0], at(z, y, c, wrap(q + d, nx)), keep=False)
        send(sa.at[y], bo.at[0], s_sib.at[0], r_sib.at[0], at(z, y, mate, q), keep=False)
        for d in range(1, nz):
            arrived(bo.at[1, up_z(nz - d)], r_op.at[d])
        for d in beside:
            send(bo.at[1], bo.at[1], s_x.at[1, d], r_x.at[1, 0], at(z, y, c, wrap(q + d, nx)), keep=False)
        send(bo.at[1], bo.at[1], s_sib.at[1], r_sib.at[1], at(z, y, mate, q), keep=False)
        bo[0] = sa[y]

    def relay(h):
        for d in beside:
            part = pl.ds(0 if d == 1 else mid, mid)

            @pl.when((c == root_c) & (away == d))
            def _():
                arrived(bo.at[h], r_x.at[h, 0])
                if nx > 2:
                    there = wrap(root_q + 2, nx)
                    view = bo.at[h, part]
                    send(view, view, s_x.at[h, 2], r_x.at[h, d], at(z, y, c, there), keep=False)
                send(bo.at[h], bo.at[h], s_sib.at[h], r_sib.at[h], at(z, y, mate, q), keep=False)

    def relay_far(h):
        if nx > 2:

            @pl.when((c == root_c) & (away == 2))
            def _():
                for d in beside:
                    view = bo.at[h, pl.ds(0 if d == 1 else mid, mid)]
                    arrived(view, r_x.at[h, d])
                send(bo.at[h], bo.at[h], s_sib.at[h], r_sib.at[h], at(z, y, mate, q), keep=False)

    wide = 2 * nz * 8
    half_wide = wide // 2

    now_ready = [False]

    def columns_ready():
        @pl.when(c != root_c)
        def _():
            for h in (0, 1):
                arrived(bo.at[h], r_sib.at[h])

        for k, e in enumerate(orders[0]):
            bn[wrap(z + nz - e, nz)] = bo[0, k]
        b_high, b_low = halves(jnp.concatenate([flat(bn[...]), flat(bo[1])], axis=0))
        b2[:, :wide] = b_high.T
        b2[:, wide:] = b_low.T

    def ready_now():
        columns_ready()
        now_ready[0] = True

    def tail_relays():
        for name in ("relay0", "relay1", "far0", "far1"):
            if name not in acted:
                act_of[name]()
        ready_now()

    acted = set()

    def once(name, act):
        def run():
            if name not in acted:
                acted.add(name)
                act()

        return run

    act_of = {
        "relay0": once("relay0", lambda: relay(0)),
        "relay1": once("relay1", lambda: relay(1)),
        "far0": once("far0", lambda: relay_far(0)),
        "far1": once("far1", lambda: relay_far(1)),
        "ready": once("ready", tail_relays),
    }

    units = 2 * ny * wide
    first = q * units + c * (ny * wide)
    col = (z * ny + y) * wide + lax.broadcasted_iota(jnp.int32, (1, wide), 1)
    inverse = 1.0 / total
    weight = ridge[0, 0]
    line8 = lax.broadcasted_iota(jnp.int32, (8, 1), 0)

    def emit(group):
        pieces, rows_of = [], []
        for which, d in group:
            n, mine = (ny, y) if which == 0 else (nz, z)
            chunk = wrap(mine + d, n)
            value = flat(sa[chunk] if which == 0 else sb[chunk])
            pieces += halves(value)
            rows_of.append((which, chunk, value.shape[0]))
        made = jnp.dot(jnp.concatenate(pieces, axis=0), b2[...], preferred_element_type=jnp.float32)
        made = made[:, :wide] + made[:, wide:]
        at_row = 0
        for which, chunk, high in rows_of:
            part = (made[at_row : at_row + high] + made[at_row + high : at_row + 2 * high]) * inverse
            at_row += 2 * high
            for k, e in enumerate(orders[which]):
                if which == 0:
                    block, zz = chunk, wrap(z + nz - e, nz)
                else:
                    block, zz = wrap(y + ny - e, ny), chunk
                unit = first + block * wide + which * half_wide + zz * 8 + line8
                ob[block, which, zz] = part[k * 8 : (k + 1) * 8] + jnp.where(unit == col, weight, 0.0)

    work = [(1, 0), (0, 0)]
    for d in range(1, max(ny, nz) // 2):
        for which in (1, 0):
            if d < extent[which] // 2:
                work += [(which, d), (which, extent[which] - d)]

    top = max(ny, nz) // 2
    done = 0
    for d in range(1, top + 1):
        for k in range(subs):
            for which in (0, 1):
                if d <= extent[which] // 2:
                    take(which, d, k)
            for now, act in PLAN:
                if now == (d, k):
                    act_of[act]()
            able = [w for w in work[done:] if min(w[1], extent[w[0]] - w[1]) < d]
            if now_ready[0] and able:
                emit(able[:GROUP])
                done += len(able[:GROUP])
    if not now_ready[0]:
        act_of["ready"]()
    while done < len(work):
        emit(work[done : done + GROUP])
        done += GROUP
    emit([(which, extent[which] // 2) for which in (1, 0)])

    for k in range(ny):
        turned = ob[k].reshape(wide, wide).T
        left, right = turned[:half_wide], turned[half_wide:]
        lanes = pl.ds(pl.multiple_of((c * ny + k) * wide, wide), wide)
        st[k] = jnp.where(c == 0, right, left)
        send(st.at[k], out.at[:, lanes], s_out.at[k], r_out.at[k], at(z, y, mate, q))
        out[:, lanes] = jnp.where(c == 0, left, right)
    for k in range(ny):
        lanes = pl.ds(pl.multiple_of((mate * ny + k) * wide, wide), wide)
        arrived(out.at[:, lanes], r_out.at[k])

    for copy in pending:
        copy.wait_send()
    for d in range(1, nz):
        for cc in (0, 1):
            sent(ra.at[0, 0], s_raw.at[0, d, cc])
    for d in range(1, ny):
        for cc in (0, 1):
            sent(rb.at[0, 0], s_raw.at[1, d, cc])

    @pl.when(c == 0)
    def _():
        sent(sm1.at[0, 0], s_sm1.at[0])

    @pl.when(c == 1)
    def _():
        for d in range(1, ny):
            for cc in (0, 1):
                sent(sm2.at[0], s_sm2.at[d, cc])
        sent(sm2.at[0], s_sm2.at[0, 0])

    @pl.when(hop != 0)
    def _():
        sent(sb.at[z, 0], s_op.at[hop])

    @pl.when((c == root_c) & (away == 0))
    def _():
        for h in (0, 1):
            for d in beside:
                sent(bo.at[h], s_x.at[h, d])

    if nx > 2:

        @pl.when((c == root_c) & (wrap(away, 2) == 1))
        def _():
            for h in (0, 1):
                sent(bo.at[h, pl.ds(0, mid)], s_x.at[h, 2])

    @pl.when(c == root_c)
    def _():
        for h in (0, 1):
            sent(bo.at[h], s_sib.at[h])


def body(hidden_panel, row_signs, sample_rows, sample_counts, ridge_weight):
    nx = lax.axis_size("cols")
    nz = 2 * nx
    ny = lax.axis_size("rows") // (2 * nz)
    width, length = hidden_panel.shape
    shards = sample_counts.shape[0]
    cap = -(-shards * sample_rows.shape[1] // 128) * 128
    half_wide = 8 * nz
    dma, f32, i32, bf16 = pltpu.SemaphoreType.DMA, jnp.float32, jnp.int32, jnp.bfloat16
    m = max(nz, ny)
    vmem = pl.BlockSpec(memory_space=pltpu.VMEM)
    smem = pl.BlockSpec(memory_space=pltpu.SMEM)
    hbm = pl.BlockSpec(memory_space=pl.ANY)
    result = pl.pallas_call(
        functools.partial(kernel, nz, ny, nx, cap),
        out_shape=pltpu.VMEM((half_wide, width), f32),
        in_specs=[hbm, vmem, smem, vmem, smem],
        out_specs=vmem,
        scratch_shapes=[
            pltpu.VMEM((2, ny, 2, nz, 8, length), f32),
            pltpu.VMEM((nz, 2, ny, 8, length), f32),
            pltpu.VMEM((ny, 2, nz, 8, length), f32),
            pltpu.VMEM((nz, 2, 1, cap), i32),
            pltpu.VMEM((ny, 1, cap), i32),
            pltpu.VMEM((ny, 8, cap), f32),
            pltpu.VMEM((nz, 8, cap), f32),
            pltpu.VMEM((ny, 8, cap), f32),
            pltpu.VMEM((nz, 8, cap), f32),
            pltpu.VMEM((ny, nz, 8, cap), f32),
            pltpu.VMEM((nz, ny, 8, cap), f32),
            pltpu.VMEM((2, nz, 8, cap), f32),
            pltpu.VMEM((nz, 8, cap), f32),
            pltpu.VMEM((cap, 4 * half_wide), bf16),
            pltpu.VMEM((2 * length, cap), bf16),
            pltpu.VMEM((ny, 2, nz, 8, 2 * half_wide), f32),
            pltpu.VMEM((ny, half_wide, 2 * half_wide), f32),
            dma(()),
            dma((2, m, 2)),
            dma((2, m, 2)),
            dma((nz,)),
            dma((nz, 2)),
            dma((ny, 2)),
            dma((ny,)),
            dma((2, m)),
            dma((2, m)),
            dma((2, m)),
            dma((2, m)),
            dma((nz,)),
            dma((nz,)),
            dma((2, nx)),
            dma((2, nx)),
            dma((2,)),
            dma((2,)),
            dma((2, 2, m // 2, m)),
            dma((2, 2, m // 2, m)),
            dma((ny,)),
            dma((ny,)),
        ],
        compiler_params=pltpu.CompilerParams(collective_id=0, has_side_effects=True),
        name="sketch_gram",
    )(
        hidden_panel.reshape(2, ny, 2, nz, 8, length),
        row_signs.reshape(1, length),
        sample_rows,
        sample_counts.reshape(1, shards),
        ridge_weight.reshape(1, 1),
    )
    return result.T


def solution(mesh):
    placed = (P("cols", "rows"), P("rows"), P("rows", None), P(), P())
    return jax.shard_map(
        body, mesh=mesh, in_specs=placed, out_specs=P("cols", "rows"), check_vma=False
    )
```

```python
import functools
import math

import jax
import jax.numpy as jnp
from jax import lax
from jax.experimental import pallas as pl
from jax.experimental.pallas import tpu as pltpu
from jax.sharding import PartitionSpec as P

MESH = pl.DeviceIdType.MESH


def halves(value):
    high = value.astype(jnp.bfloat16)
    return high, (value - high.astype(jnp.float32)).astype(jnp.bfloat16)


def wrap(value, n):
    return value & (n - 1) if n & (n - 1) == 0 else lax.rem(value, n)


def signs_of(common):
    for shift in (8, 4, 2, 1):
        common = common ^ (common >> shift)
    return (1 - 2 * (common & 1)).astype(jnp.float32)


def far_first(n):
    return [n // 2] + [d for k in range(n // 2 - 1, 0, -1) for d in (k, n - k)]


def near_first(n):
    return [d for k in range(1, n // 2) for d in (k, n - k)] + [n // 2]


SUBS = 4
GROUP = 4
PLAN = (((1, 2), "relay0"), ((1, 3), "relay1"), ((2, 0), "far0"), ((2, 2), "far1"), ((2, 3), "ready"))


def kernel(
    nz, ny, nx, cap, panel, signs, rows, counts, ridge, out,
    xs, ra, rb, sm1, sm2, pa, pb, qa, qb, sa, sb, bo, bn, b2, hh, ob, st,
    in_sem, s_raw, r_raw, s_sm1, r_sm1, s_sm2, r_sm2, s_red, r_red, s_ag, r_ag,
    s_op, r_op, s_x, r_x, s_sib, r_sib, s_ring, r_ring, s_out, r_out,
):
    length = panel.shape[-1]
    shards = counts.shape[1]
    me = lax.axis_index("rows")
    q = lax.axis_index("cols")
    c = wrap(me, 2)
    y = wrap(me >> 1, ny)
    z = (me >> 1) // ny if ny & (ny - 1) else me >> ny.bit_length()
    mate = 1 - c

    def at(zz, yy, cc, xx):
        return ((zz * ny + yy) * 2 + cc, xx)

    def up_z(d):
        return wrap(z + d, nz)

    def up_y(d):
        return wrap(y + d, ny)

    def send(src, dst, ss, rs, to):
        pltpu.make_async_remote_copy(
            src_ref=src, dst_ref=dst, send_sem=ss, recv_sem=rs, device_id=to, device_id_type=MESH
        ).start()

    def arrived(slot, sem):
        pltpu.make_async_copy(slot, slot, sem).wait()

    def sent(src, sem):
        pltpu.make_async_copy(src, src, sem).wait()

    load = pltpu.make_async_copy(panel, xs, in_sem)
    load.start()

    barrier = pltpu.get_barrier_semaphore()
    greeted = [at(z, y, mate, q)]
    for d in range(1, nz):
        greeted += [at(up_z(d), y, cc, q) for cc in (0, 1)]
    for d in range(1, ny):
        greeted += [at(z, up_y(d), cc, q) for cc in (0, 1)]
    for d in range(1, nx):
        greeted.append(at(z, y, c, wrap(q + d, nx)))
    for to in greeted:
        pl.semaphore_signal(barrier, inc=1, device_id=to, device_id_type=MESH)

    count_row = counts[...].astype(jnp.float32)
    lane = lax.broadcasted_iota(jnp.int32, (shards, shards), 1)
    line = lax.broadcasted_iota(jnp.int32, (shards, shards), 0)
    ends = jnp.sum(jnp.where(lane <= line, count_row, 0.0), axis=1, keepdims=True)
    slot = lax.broadcasted_iota(jnp.int32, (1, cap), 1)
    passed = ends <= slot.astype(jnp.float32)
    pk = jnp.sum(passed.astype(jnp.float32), axis=0, keepdims=True).astype(jnp.int32)
    block = lax.broadcasted_iota(jnp.int32, (1, shards), 1)
    before = jnp.sum(jnp.where(block < me, count_row, 0.0), axis=1, keepdims=True)
    total = jnp.sum(count_row, axis=1, keepdims=True)
    place = slot - before.astype(jnp.int32)
    own = jnp.zeros((1, cap), jnp.int32)
    for j in range(rows.shape[1]):
        own = jnp.where((pk == me) & (place == j), rows[0, j] - me * length, own)
    sm1[z, c] = own

    load.wait()
    xs[...] = xs[...] * signs[...]
    pl.semaphore_wait(barrier, len(greeted))

    @pl.when(c == 0)
    def _():
        send(sm1.at[z, 0], sm1.at[z, 0], s_sm1.at[0], r_sm1.at[0, 0], at(z, y, 1, q))

    for d in range(1, nz):
        send(sm1.at[z, c], sm1.at[z, c], s_sm1.at[1], r_sm1.at[d, c], at(up_z(d), y, 1, q))

    def raw_z(d):
        for cc in (0, 1):
            send(xs.at[cc, :, 0, up_z(d)], ra.at[z, c], s_raw.at[0, 0], r_raw.at[0, d, c], at(up_z(d), y, cc, q))

    def raw_y(d):
        for cc in (0, 1):
            send(xs.at[cc, up_y(d), 1], rb.at[y, c], s_raw.at[1, 0], r_raw.at[1, d, c], at(z, up_y(d), cc, q))

    send(xs.at[mate, :, 0, z], ra.at[z, c], s_raw.at[0, 1], r_raw.at[0, 0, c], at(z, y, mate, q))
    send(xs.at[mate, y, 1], rb.at[y, c], s_raw.at[1, 1], r_raw.at[1, 0, c], at(z, y, mate, q))

    order_z, order_y = near_first(nz), near_first(ny)

    @pl.when(c == 0)
    def _():
        for k in range(max(len(order_z), len(order_y))):
            if k < len(order_z):
                raw_z(order_z[k])
            if k < len(order_y):
                raw_y(order_y[k])

    @pl.when(c == 1)
    def _():
        for d in order_z:
            raw_z(d)
        arrived(sm1.at[z, 0], r_sm1.at[0, 0])
        for d in range(1, nz):
            for cc in (0, 1):
                arrived(sm1.at[up_z(nz - d), cc], r_sm1.at[d, cc])
        sm2[y] = jnp.sum(sm1[...].reshape(2 * nz, 1, cap), axis=0)
        for d in range(1, ny):
            for cc in (0, 1):
                send(sm2.at[y], sm2.at[y], s_sm2.at[1 + cc], r_sm2.at[d], at(z, up_y(d), cc, q))
        send(sm2.at[y], sm2.at[y], s_sm2.at[0], r_sm2.at[0], at(z, y, 0, q))
        for d in order_y:
            raw_y(d)

    @pl.when(c == 0)
    def _():
        arrived(sm2.at[y], r_sm2.at[0])

    for d in range(1, ny):
        arrived(sm2.at[up_y(ny - d)], r_sm2.at[d])
    local_row = jnp.sum(sm2[...], axis=0)

    token = lax.broadcasted_iota(jnp.int32, (length, cap), 0)
    scale = 1.0 / math.sqrt(length * shards)
    live = jnp.where(slot.astype(jnp.float32) < total, scale, 0.0)
    sign = (signs_of(token & local_row) * live).astype(jnp.bfloat16)
    hh[:length] = sign
    hh[length:] = sign

    def share(parts, acc):
        pieces = [jnp.concatenate(halves(value), axis=1) for value, _ in parts]
        made = jnp.dot(jnp.concatenate(pieces, axis=0), hh[...], preferred_element_type=jnp.float32)
        high = made.shape[0] // len(parts)
        for k, (_, source) in enumerate(parts):
            term = made[k * high : (k + 1) * high] * signs_of(pk & source)
            acc = term if acc is None else acc + term
        return acc

    def batches(n):
        return [(0,)] + [(d, n - d) for d in range(1, n // 2)] + [(n // 2,)]

    def flat(value):
        return value.reshape(-1, value.shape[-1])

    def block_of(zz, yy, cc):
        return (zz * ny + yy) * 2 + cc

    def share_of(which, batch, acc):
        n, mine, buf = (nz, z, ra) if which == 0 else (ny, y, rb)
        parts = []
        for d in batch:
            far = wrap(mine + n - d, n) if d else mine
            for cc in (0, 1):
                if d == 0 and cc == 0:
                    held = xs[c, :, 0, z] if which == 0 else xs[c, y, 1]
                    parts.append((flat(held), block_of(z, y, c)))
                    continue
                source = mate if d == 0 else cc
                arrived(buf.at[far, source], r_raw.at[which, d, source])
                block_at = block_of(far, y, source) if which == 0 else block_of(z, far, source)
                parts.append((flat(buf[far, source]), block_at))
        return share(parts, acc)

    steps_z, steps_y = batches(nz), batches(ny)
    acc_z = acc_y = None
    for k in range(max(len(steps_z), len(steps_y))):
        if k < len(steps_z):
            acc_z = share_of(0, steps_z[k], acc_z)
            if k == len(steps_z) - 1:
                pa[...] = acc_z.reshape(ny, 8, cap)
                for d in far_first(ny):
                    send(pa.at[up_y(d)], qa.at[y], s_red.at[0], r_red.at[0], at(z, up_y(d), c, q))
        if k < len(steps_y):
            acc_y = share_of(1, steps_y[k], acc_y)
            if k == len(steps_y) - 1:
                pb[...] = acc_y.reshape(nz, 8, cap)
                for d in far_first(nz):
                    send(pb.at[up_z(d)], qb.at[z], s_red.at[1], r_red.at[1], at(up_z(d), y, c, q))

    subs = min(SUBS, nz, ny)

    def hold(which, d, k):
        n, mine, buf = (ny, y, sa) if which == 0 else (nz, z, sb)
        size = buf.shape[1] // subs
        return buf.at[wrap(mine + d, n), pl.ds(k * size, size)]

    extent = (ny, nz)
    orders = ([0] + near_first(nz), [0] + near_first(ny))

    def come_from(which, way, d):
        return (extent[which] - d) % extent[which] if way == 0 else d

    def passes(which, way, d, k):
        n = extent[which]
        return d < n // 2 or (d == n // 2 and k % 2 == way)

    def pass_on(which, d, k, ways=(0, 1)):
        n = extent[which]
        leap = min(2, n // 2)
        for way in ways:
            view = hold(which, come_from(which, way, d), k)
            for far in ([d + 1] if d + 1 < n // 2 else []) + ([n // 2] if d == n // 2 - leap else []):
                if not passes(which, way, far, k):
                    continue
                step = far - d if way == 0 else n - (far - d)
                to = at(z, up_y(step), c, q) if which == 0 else at(up_z(step), y, c, q)
                send(view, view, s_ring.at[which], r_ring.at[which, way, far - 1, k], to)

    def take(which, d, k):
        for way in (0, 1):
            if passes(which, way, d, k):
                view = hold(which, come_from(which, way, d), k)
                arrived(view, r_ring.at[which, way, d - 1, k])
                pass_on(which, d, k, (way,))

    target = 2 * q + c
    hop = wrap(target - z + nz, nz)

    piece = pa[y]
    arrived(qa.at[pl.ds(0, ny - 1)], r_red.at[0])
    for d in range(1, ny):
        piece = piece + qa[up_y(ny - d)]
    sa[y, 0] = piece
    for d in near_first(nz):
        send(sa.at[y, 0], sa.at[y, orders[0].index(d)], s_ag.at[0], r_ag.at[0, d], at(up_z(d), y, c, q))
    piece = pb[z]
    arrived(qb.at[pl.ds(0, nz - 1)], r_red.at[1])
    for d in range(1, nz):
        piece = piece + qb[up_z(nz - d)]
    sb[z, 0] = piece

    @pl.when(hop != 0)
    def _():
        send(sb.at[z, 0], bo.at[1, z], s_op.at[hop], r_op.at[hop], at(target, y, c, q))

    @pl.when(hop == 0)
    def _():
        bo[1, z] = piece

    for d in near_first(ny):
        send(sb.at[z, 0], sb.at[z, orders[1].index(d)], s_ag.at[1], r_ag.at[1, d], at(z, up_y(d), c, q))
    for k in range(subs):
        for which in (0, 1):
            mine, buf = (y, sa) if which == 0 else (z, sb)
            size = buf.shape[1] // subs
            for place_of in range(k * size, (k + 1) * size):
                e = orders[which][place_of]
                if e:
                    arrived(buf.at[mine, place_of], r_ag.at[which, e])
            pass_on(which, 0, k)

    root_c = wrap(z, 2)
    root_q = z >> 1
    away = wrap(q - root_q + nx, nx)
    beside = [d for d in (1, nx - 1) if d] if nx > 2 else [1]
    mid = nz // 2

    @pl.when((c == root_c) & (away == 0))
    def _():
        for d in beside:
            send(sa.at[y], bo.at[0], s_x.at[0, d], r_x.at[0, 0], at(z, y, c, wrap(q + d, nx)))
        send(sa.at[y], bo.at[0], s_sib.at[0], r_sib.at[0], at(z, y, mate, q))
        for d in range(1, nz):
            arrived(bo.at[1, up_z(nz - d)], r_op.at[d])
        for d in beside:
            send(bo.at[1], bo.at[1], s_x.at[1, d], r_x.at[1, 0], at(z, y, c, wrap(q + d, nx)))
        send(bo.at[1], bo.at[1], s_sib.at[1], r_sib.at[1], at(z, y, mate, q))
        bo[0] = sa[y]

    def relay(h):
        for d in beside:
            part = pl.ds(0 if d == 1 else mid, mid)

            @pl.when((c == root_c) & (away == d))
            def _():
                arrived(bo.at[h], r_x.at[h, 0])
                if nx > 2:
                    there = wrap(root_q + 2, nx)
                    view = bo.at[h, part]
                    send(view, view, s_x.at[h, 2], r_x.at[h, d], at(z, y, c, there))
                send(bo.at[h], bo.at[h], s_sib.at[h], r_sib.at[h], at(z, y, mate, q))

    def relay_far(h):
        if nx > 2:

            @pl.when((c == root_c) & (away == 2))
            def _():
                for d in beside:
                    view = bo.at[h, pl.ds(0 if d == 1 else mid, mid)]
                    arrived(view, r_x.at[h, d])
                send(bo.at[h], bo.at[h], s_sib.at[h], r_sib.at[h], at(z, y, mate, q))

    wide = 2 * nz * 8
    half_wide = wide // 2

    now_ready = [False]

    def columns_ready():
        @pl.when(c != root_c)
        def _():
            for h in (0, 1):
                arrived(bo.at[h], r_sib.at[h])

        for k, e in enumerate(orders[0]):
            bn[wrap(z + nz - e, nz)] = bo[0, k]
        b_high, b_low = halves(jnp.concatenate([flat(bn[...]), flat(bo[1])], axis=0))
        b2[:, :wide] = b_high.T
        b2[:, wide:] = b_low.T

    def ready_now():
        columns_ready()
        now_ready[0] = True

    def tail_relays():
        for name in ("relay0", "relay1", "far0", "far1"):
            if name not in acted:
                act_of[name]()
        ready_now()

    acted = set()

    def once(name, act):
        def run():
            if name not in acted:
                acted.add(name)
                act()

        return run

    act_of = {
        "relay0": once("relay0", lambda: relay(0)),
        "relay1": once("relay1", lambda: relay(1)),
        "far0": once("far0", lambda: relay_far(0)),
        "far1": once("far1", lambda: relay_far(1)),
        "ready": once("ready", tail_relays),
    }

    units = 2 * ny * wide
    first = q * units + c * (ny * wide)
    col = (z * ny + y) * wide + lax.broadcasted_iota(jnp.int32, (1, wide), 1)
    inverse = 1.0 / total
    weight = ridge[0, 0]
    line8 = lax.broadcasted_iota(jnp.int32, (8, 1), 0)

    def emit(group):
        pieces, rows_of = [], []
        for which, d in group:
            n, mine = (ny, y) if which == 0 else (nz, z)
            chunk = wrap(mine + d, n)
            value = flat(sa[chunk] if which == 0 else sb[chunk])
            pieces += halves(value)
            rows_of.append((which, chunk, value.shape[0]))
        made = jnp.dot(jnp.concatenate(pieces, axis=0), b2[...], preferred_element_type=jnp.float32)
        made = made[:, :wide] + made[:, wide:]
        at_row = 0
        for which, chunk, high in rows_of:
            part = (made[at_row : at_row + high] + made[at_row + high : at_row + 2 * high]) * inverse
            at_row += 2 * high
            for k, e in enumerate(orders[which]):
                if which == 0:
                    block, zz = chunk, wrap(z + nz - e, nz)
                else:
                    block, zz = wrap(y + ny - e, ny), chunk
                unit = first + block * wide + which * half_wide + zz * 8 + line8
                ob[block, which, zz] = part[k * 8 : (k + 1) * 8] + jnp.where(unit == col, weight, 0.0)

    work = [(1, 0), (0, 0)]
    for d in range(1, max(ny, nz) // 2):
        for which in (1, 0):
            if d < extent[which] // 2:
                work += [(which, d), (which, extent[which] - d)]

    top = max(ny, nz) // 2
    done = 0
    for d in range(1, top + 1):
        for k in range(subs):
            for which in (0, 1):
                if d <= extent[which] // 2:
                    take(which, d, k)
            for now, act in PLAN:
                if now == (d, k):
                    act_of[act]()
            able = [w for w in work[done:] if min(w[1], extent[w[0]] - w[1]) < d]
            if now_ready[0] and able:
                emit(able[:GROUP])
                done += len(able[:GROUP])
    if not now_ready[0]:
        act_of["ready"]()
    while done < len(work):
        emit(work[done : done + GROUP])
        done += GROUP
    emit([(which, extent[which] // 2) for which in (1, 0)])

    for k in range(ny):
        turned = ob[k].reshape(wide, wide).T
        left, right = turned[:half_wide], turned[half_wide:]
        lanes = pl.ds(pl.multiple_of((c * ny + k) * wide, wide), wide)
        st[k] = jnp.where(c == 0, right, left)
        send(st.at[k], out.at[:, lanes], s_out, r_out, at(z, y, mate, q))
        out[:, lanes] = jnp.where(c == 0, left, right)
    for which, n, raw, red, buf in ((0, nz, ra, qa, sa), (1, ny, rb, qb, sb)):
        sent(raw.at[pl.ds(0, n - 1)], s_raw.at[which, 0])
        sent(raw.at[0, 0], s_raw.at[which, 1])
        sent(red.at[pl.ds(0, red.shape[0] - 1)], s_red.at[which])
        sent(buf.at[0, pl.ds(0, n - 1)], s_ag.at[which])
        sent(buf.at[pl.ds(0, buf.shape[0] - 1)], s_ring.at[which])
    sent(sm1.at[pl.ds(0, nz - 1), 0], s_sm1.at[1])

    @pl.when(c == 0)
    def _():
        sent(sm1.at[0, 0], s_sm1.at[0])

    @pl.when(c == 1)
    def _():
        for cc in (0, 1):
            sent(sm2.at[pl.ds(0, ny - 1)], s_sm2.at[1 + cc])
        sent(sm2.at[0], s_sm2.at[0])

    @pl.when(hop != 0)
    def _():
        sent(sb.at[z, 0], s_op.at[hop])

    @pl.when((c == root_c) & (away == 0))
    def _():
        for h in (0, 1):
            for d in beside:
                sent(bo.at[h], s_x.at[h, d])

    if nx > 2:

        @pl.when((c == root_c) & (wrap(away, 2) == 1))
        def _():
            for h in (0, 1):
                sent(bo.at[h, pl.ds(0, mid)], s_x.at[h, 2])

    @pl.when(c == root_c)
    def _():
        for h in (0, 1):
            sent(bo.at[h], s_sib.at[h])

    sent(st, s_out)
    arrived(out.at[:, pl.ds(pl.multiple_of(mate * (ny * wide), wide), ny * wide)], r_out)


def body(hidden_panel, row_signs, sample_rows, sample_counts, ridge_weight):
    nx = lax.axis_size("cols")
    nz = 2 * nx
    ny = lax.axis_size("rows") // (2 * nz)
    width, length = hidden_panel.shape
    shards = sample_counts.shape[0]
    cap = -(-shards * sample_rows.shape[1] // 128) * 128
    half_wide = 8 * nz
    dma, f32, i32, bf16 = pltpu.SemaphoreType.DMA, jnp.float32, jnp.int32, jnp.bfloat16
    m = max(nz, ny)
    vmem = pl.BlockSpec(memory_space=pltpu.VMEM)
    smem = pl.BlockSpec(memory_space=pltpu.SMEM)
    hbm = pl.BlockSpec(memory_space=pl.ANY)
    result = pl.pallas_call(
        functools.partial(kernel, nz, ny, nx, cap),
        out_shape=pltpu.VMEM((half_wide, width), f32),
        in_specs=[hbm, vmem, smem, vmem, smem],
        out_specs=vmem,
        scratch_shapes=[
            pltpu.VMEM((2, ny, 2, nz, 8, length), f32),
            pltpu.VMEM((nz, 2, ny, 8, length), f32),
            pltpu.VMEM((ny, 2, nz, 8, length), f32),
            pltpu.VMEM((nz, 2, 1, cap), i32),
            pltpu.VMEM((ny, 1, cap), i32),
            pltpu.VMEM((ny, 8, cap), f32),
            pltpu.VMEM((nz, 8, cap), f32),
            pltpu.VMEM((ny, 8, cap), f32),
            pltpu.VMEM((nz, 8, cap), f32),
            pltpu.VMEM((ny, nz, 8, cap), f32),
            pltpu.VMEM((nz, ny, 8, cap), f32),
            pltpu.VMEM((2, nz, 8, cap), f32),
            pltpu.VMEM((nz, 8, cap), f32),
            pltpu.VMEM((cap, 4 * half_wide), bf16),
            pltpu.VMEM((2 * length, cap), bf16),
            pltpu.VMEM((ny, 2, nz, 8, 2 * half_wide), f32),
            pltpu.VMEM((ny, half_wide, 2 * half_wide), f32),
            dma(()),
            dma((2, 2)),
            dma((2, m, 2)),
            dma((2,)),
            dma((nz, 2)),
            dma((3,)),
            dma((ny,)),
            dma((2,)),
            dma((2,)),
            dma((2,)),
            dma((2, m)),
            dma((nz,)),
            dma((nz,)),
            dma((2, nx)),
            dma((2, nx)),
            dma((2,)),
            dma((2,)),
            dma((2,)),
            dma((2, 2, m // 2, m)),
            dma(()),
            dma(()),
        ],
        compiler_params=pltpu.CompilerParams(collective_id=0, has_side_effects=True),
        name="sketch_gram",
    )(
        hidden_panel.reshape(2, ny, 2, nz, 8, length),
        row_signs.reshape(1, length),
        sample_rows,
        sample_counts.reshape(1, shards),
        ridge_weight.reshape(1, 1),
    )
    return result.T


def solution(mesh):
    placed = (P("cols", "rows"), P("rows"), P("rows", None), P(), P())
    return jax.shard_map(
        body, mesh=mesh, in_specs=placed, out_specs=P("cols", "rows"), check_vma=False
    )
```

```python
import functools
import math

import jax
import jax.numpy as jnp
from jax import lax
from jax.experimental import pallas as pl
from jax.experimental.pallas import tpu as pltpu
from jax.sharding import PartitionSpec as P

MESH = pl.DeviceIdType.MESH


def halves(value):
    high = value.astype(jnp.bfloat16)
    return high, (value - high.astype(jnp.float32)).astype(jnp.bfloat16)


def wrap(value, n):
    return value & (n - 1) if n & (n - 1) == 0 else lax.rem(value, n)


def signs_of(common):
    for shift in (8, 4, 2, 1):
        common = common ^ (common >> shift)
    return (1 - 2 * (common & 1)).astype(jnp.float32)


def far_first(n):
    return [n // 2] + [d for k in range(n // 2 - 1, 0, -1) for d in (k, n - k)]


def near_first(n):
    return [d for k in range(1, n // 2) for d in (k, n - k)] + [n // 2]


SUBS = 4
GROUP = 4
PLAN = (((1, 2), "relay0"), ((1, 3), "relay1"), ((2, 0), "far0"), ((2, 2), "far1"), ((2, 3), "ready"))


def kernel(
    nz, ny, nx, cap, panel, signs, rows, counts, ridge, out,
    xs, ra, rb, sm1, sm2, pa, pb, qa, qb, sa, sb, bo, bn, b2, hh, ob, st,
    in_sem, s_raw, r_raw, s_sm1, r_sm1, s_sm2, r_sm2, s_red, r_red, s_ag, r_ag,
    s_op, r_op, s_x, r_x, s_sib, r_sib, s_ring, r_ring, s_out, r_out,
):
    length = panel.shape[-1]
    shards = counts.shape[1]
    me = lax.axis_index("rows")
    q = lax.axis_index("cols")
    c = wrap(me, 2)
    y = wrap(me >> 1, ny)
    z = (me >> 1) // ny if ny & (ny - 1) else me >> ny.bit_length()
    mate = 1 - c

    def at(zz, yy, cc, xx):
        return ((zz * ny + yy) * 2 + cc, xx)

    def up_z(d):
        return wrap(z + d, nz)

    def up_y(d):
        return wrap(y + d, ny)

    def send(src, dst, ss, rs, to):
        pltpu.make_async_remote_copy(
            src_ref=src, dst_ref=dst, send_sem=ss, recv_sem=rs, device_id=to, device_id_type=MESH
        ).start()

    def arrived(slot, sem):
        pltpu.make_async_copy(slot, slot, sem).wait()

    def sent(src, sem):
        pltpu.make_async_copy(src, src, sem).wait()

    load = pltpu.make_async_copy(panel, xs, in_sem)
    load.start()

    barrier = pltpu.get_barrier_semaphore()
    greeted = [at(z, y, mate, q)]
    for d in range(1, nz):
        greeted += [at(up_z(d), y, cc, q) for cc in (0, 1)]
    for d in range(1, ny):
        greeted += [at(z, up_y(d), cc, q) for cc in (0, 1)]
    for d in range(1, nx):
        greeted.append(at(z, y, c, wrap(q + d, nx)))
    for to in greeted:
        pl.semaphore_signal(barrier, inc=1, device_id=to, device_id_type=MESH)

    count_row = counts[...].astype(jnp.float32)
    lane = lax.broadcasted_iota(jnp.int32, (shards, shards), 1)
    line = lax.broadcasted_iota(jnp.int32, (shards, shards), 0)
    ends = jnp.sum(jnp.where(lane <= line, count_row, 0.0), axis=1, keepdims=True)
    slot = lax.broadcasted_iota(jnp.int32, (1, cap), 1)
    passed = ends <= slot.astype(jnp.float32)
    pk = jnp.sum(passed.astype(jnp.float32), axis=0, keepdims=True).astype(jnp.int32)
    block = lax.broadcasted_iota(jnp.int32, (1, shards), 1)
    before = jnp.sum(jnp.where(block < me, count_row, 0.0), axis=1, keepdims=True)
    total = jnp.sum(count_row, axis=1, keepdims=True)
    place = slot - before.astype(jnp.int32)
    own = jnp.zeros((1, cap), jnp.int32)
    for j in range(rows.shape[1]):
        own = jnp.where((pk == me) & (place == j), rows[0, j] - me * length, own)
    sm1[z, c] = own

    load.wait()
    xs[...] = xs[...] * signs[...]
    pl.semaphore_wait(barrier, len(greeted))

    @pl.when(c == 0)
    def _():
        send(sm1.at[z, 0], sm1.at[z, 0], s_sm1.at[0], r_sm1.at[0], at(z, y, 1, q))

    for d in range(1, nz):
        send(sm1.at[z, c], sm1.at[z, c], s_sm1.at[1], r_sm1.at[1], at(up_z(d), y, 1, q))

    def raw_z(d):
        for cc in (0, 1):
            send(xs.at[cc, :, 0, up_z(d)], ra.at[z, c], s_raw.at[0, 0], r_raw.at[0, d], at(up_z(d), y, cc, q))

    def raw_y(d):
        for cc in (0, 1):
            send(xs.at[cc, up_y(d), 1], rb.at[y, c], s_raw.at[1, 0], r_raw.at[1, d], at(z, up_y(d), cc, q))

    send(xs.at[mate, :, 0, z], ra.at[z, c], s_raw.at[0, 1], r_raw.at[0, 0], at(z, y, mate, q))
    send(xs.at[mate, y, 1], rb.at[y, c], s_raw.at[1, 1], r_raw.at[1, 0], at(z, y, mate, q))

    order_z, order_y = near_first(nz), near_first(ny)

    @pl.when(c == 0)
    def _():
        for k in range(max(len(order_z), len(order_y))):
            if k < len(order_z):
                raw_z(order_z[k])
            if k < len(order_y):
                raw_y(order_y[k])

    @pl.when(c == 1)
    def _():
        for d in order_z:
            raw_z(d)
        arrived(sm1.at[z, 0], r_sm1.at[0])
        arrived(sm1.at[pl.ds(0, nz - 1)], r_sm1.at[1])
        sm2[y] = jnp.sum(sm1[...].reshape(2 * nz, 1, cap), axis=0)
        for d in range(1, ny):
            for cc in (0, 1):
                send(sm2.at[y], sm2.at[y], s_sm2.at[1 + cc], r_sm2.at[1], at(z, up_y(d), cc, q))
        send(sm2.at[y], sm2.at[y], s_sm2.at[0], r_sm2.at[0], at(z, y, 0, q))
        for d in order_y:
            raw_y(d)

    @pl.when(c == 0)
    def _():
        arrived(sm2.at[y], r_sm2.at[0])

    arrived(sm2.at[pl.ds(0, ny - 1)], r_sm2.at[1])
    local_row = jnp.sum(sm2[...], axis=0)

    token = lax.broadcasted_iota(jnp.int32, (length, cap), 0)
    scale = 1.0 / math.sqrt(length * shards)
    live = jnp.where(slot.astype(jnp.float32) < total, scale, 0.0)
    sign = (signs_of(token & local_row) * live).astype(jnp.bfloat16)
    hh[:length] = sign
    hh[length:] = sign

    def share(parts, acc):
        pieces = [jnp.concatenate(halves(value), axis=1) for value, _ in parts]
        made = jnp.dot(jnp.concatenate(pieces, axis=0), hh[...], preferred_element_type=jnp.float32)
        high = made.shape[0] // len(parts)
        for k, (_, source) in enumerate(parts):
            term = made[k * high : (k + 1) * high] * signs_of(pk & source)
            acc = term if acc is None else acc + term
        return acc

    def batches(n):
        return [(0,)] + [(d, n - d) for d in range(1, n // 2)] + [(n // 2,)]

    def flat(value):
        return value.reshape(-1, value.shape[-1])

    def block_of(zz, yy, cc):
        return (zz * ny + yy) * 2 + cc

    def share_of(which, batch, acc):
        n, mine, buf = (nz, z, ra) if which == 0 else (ny, y, rb)
        parts = []
        for d in batch:
            far = wrap(mine + n - d, n) if d else mine
            for cc in (0, 1):
                if d == 0 and cc == 0:
                    held = xs[c, :, 0, z] if which == 0 else xs[c, y, 1]
                    parts.append((flat(held), block_of(z, y, c)))
                    continue
                source = mate if d == 0 else cc
                if cc == 0:
                    arrived(buf.at[far], r_raw.at[which, d])
                elif d == 0:
                    arrived(buf.at[far, source], r_raw.at[which, 0])
                block_at = block_of(far, y, source) if which == 0 else block_of(z, far, source)
                parts.append((flat(buf[far, source]), block_at))
        return share(parts, acc)

    steps_z, steps_y = batches(nz), batches(ny)
    acc_z = acc_y = None
    for k in range(max(len(steps_z), len(steps_y))):
        if k < len(steps_z):
            acc_z = share_of(0, steps_z[k], acc_z)
            if k == len(steps_z) - 1:
                pa[...] = acc_z.reshape(ny, 8, cap)
                for d in far_first(ny):
                    send(pa.at[up_y(d)], qa.at[y], s_red.at[0], r_red.at[0], at(z, up_y(d), c, q))
        if k < len(steps_y):
            acc_y = share_of(1, steps_y[k], acc_y)
            if k == len(steps_y) - 1:
                pb[...] = acc_y.reshape(nz, 8, cap)
                for d in far_first(nz):
                    send(pb.at[up_z(d)], qb.at[z], s_red.at[1], r_red.at[1], at(up_z(d), y, c, q))

    subs = min(SUBS, nz, ny)

    def hold(which, d, k):
        n, mine, buf = (ny, y, sa) if which == 0 else (nz, z, sb)
        size = buf.shape[1] // subs
        return buf.at[wrap(mine + d, n), pl.ds(k * size, size)]

    extent = (ny, nz)
    orders = ([0] + near_first(nz), [0] + near_first(ny))

    def come_from(which, way, d):
        return (extent[which] - d) % extent[which] if way == 0 else d

    def passes(which, way, d, k):
        n = extent[which]
        return d < n // 2 or (d == n // 2 and k % 2 == way)

    def pass_on(which, d, k, ways=(0, 1)):
        n = extent[which]
        leap = min(2, n // 2)
        for way in ways:
            view = hold(which, come_from(which, way, d), k)
            for far in ([d + 1] if d + 1 < n // 2 else []) + ([n // 2] if d == n // 2 - leap else []):
                if not passes(which, way, far, k):
                    continue
                step = far - d if way == 0 else n - (far - d)
                to = at(z, up_y(step), c, q) if which == 0 else at(up_z(step), y, c, q)
                send(view, view, s_ring.at[which], r_ring.at[which, way, far - 1, k], to)

    def take(which, d, k):
        for way in (0, 1):
            if passes(which, way, d, k):
                view = hold(which, come_from(which, way, d), k)
                arrived(view, r_ring.at[which, way, d - 1, k])
                pass_on(which, d, k, (way,))

    target = 2 * q + c
    hop = wrap(target - z + nz, nz)

    piece = pa[y]
    arrived(qa.at[pl.ds(0, ny - 1)], r_red.at[0])
    for d in range(1, ny):
        piece = piece + qa[up_y(ny - d)]
    sa[y, 0] = piece
    for d in near_first(nz):
        send(sa.at[y, 0], sa.at[y, orders[0].index(d)], s_ag.at[0], r_ag.at[0, orders[0].index(d) * subs // nz], at(up_z(d), y, c, q))
    piece = pb[z]
    arrived(qb.at[pl.ds(0, nz - 1)], r_red.at[1])
    for d in range(1, nz):
        piece = piece + qb[up_z(nz - d)]
    sb[z, 0] = piece

    @pl.when(hop != 0)
    def _():
        send(sb.at[z, 0], bo.at[1, z], s_op, r_op, at(target, y, c, q))

    @pl.when(hop == 0)
    def _():
        bo[1, z] = piece

    for d in near_first(ny):
        send(sb.at[z, 0], sb.at[z, orders[1].index(d)], s_ag.at[1], r_ag.at[1, orders[1].index(d) * subs // ny], at(z, up_y(d), c, q))
    for k in range(subs):
        for which in (0, 1):
            mine, buf = (y, sa) if which == 0 else (z, sb)
            size = buf.shape[1] // subs
            begin = max(k * size, 1)
            if begin < (k + 1) * size:
                arrived(buf.at[mine, pl.ds(begin, (k + 1) * size - begin)], r_ag.at[which, k])
            pass_on(which, 0, k)

    root_c = wrap(z, 2)
    root_q = z >> 1
    away = wrap(q - root_q + nx, nx)
    beside = [d for d in (1, nx - 1) if d] if nx > 2 else [1]
    mid = nz // 2

    @pl.when((c == root_c) & (away == 0))
    def _():
        for d in beside:
            send(sa.at[y], bo.at[0], s_x.at[0, d], r_x.at[0, 0], at(z, y, c, wrap(q + d, nx)))
        send(sa.at[y], bo.at[0], s_sib.at[0], r_sib.at[0], at(z, y, mate, q))
        arrived(bo.at[1, pl.ds(0, nz - 1)], r_op)
        for d in beside:
            send(bo.at[1], bo.at[1], s_x.at[1, d], r_x.at[1, 0], at(z, y, c, wrap(q + d, nx)))
        send(bo.at[1], bo.at[1], s_sib.at[1], r_sib.at[1], at(z, y, mate, q))
        bo[0] = sa[y]

    def relay(h):
        for d in beside:
            part = pl.ds(0 if d == 1 else mid, mid)

            @pl.when((c == root_c) & (away == d))
            def _():
                arrived(bo.at[h], r_x.at[h, 0])
                if nx > 2:
                    there = wrap(root_q + 2, nx)
                    view = bo.at[h, part]
                    send(view, view, s_x.at[h, 2], r_x.at[h, d], at(z, y, c, there))
                send(bo.at[h], bo.at[h], s_sib.at[h], r_sib.at[h], at(z, y, mate, q))

    def relay_far(h):
        if nx > 2:

            @pl.when((c == root_c) & (away == 2))
            def _():
                for d in beside:
                    view = bo.at[h, pl.ds(0 if d == 1 else mid, mid)]
                    arrived(view, r_x.at[h, d])
                send(bo.at[h], bo.at[h], s_sib.at[h], r_sib.at[h], at(z, y, mate, q))

    wide = 2 * nz * 8
    half_wide = wide // 2

    now_ready = [False]

    def columns_ready():
        @pl.when(c != root_c)
        def _():
            for h in (0, 1):
                arrived(bo.at[h], r_sib.at[h])

        for k, e in enumerate(orders[0]):
            bn[wrap(z + nz - e, nz)] = bo[0, k]
        b_high, b_low = halves(jnp.concatenate([flat(bn[...]), flat(bo[1])], axis=0))
        b2[:, :wide] = b_high.T
        b2[:, wide:] = b_low.T

    def ready_now():
        columns_ready()
        now_ready[0] = True

    def tail_relays():
        for name in ("relay0", "relay1", "far0", "far1"):
            if name not in acted:
                act_of[name]()
        ready_now()

    acted = set()

    def once(name, act):
        def run():
            if name not in acted:
                acted.add(name)
                act()

        return run

    act_of = {
        "relay0": once("relay0", lambda: relay(0)),
        "relay1": once("relay1", lambda: relay(1)),
        "far0": once("far0", lambda: relay_far(0)),
        "far1": once("far1", lambda: relay_far(1)),
        "ready": once("ready", tail_relays),
    }

    units = 2 * ny * wide
    first = q * units + c * (ny * wide)
    col = (z * ny + y) * wide + lax.broadcasted_iota(jnp.int32, (1, wide), 1)
    inverse = 1.0 / total
    weight = ridge[0, 0]
    line8 = lax.broadcasted_iota(jnp.int32, (8, 1), 0)

    def emit(group):
        pieces, rows_of = [], []
        for which, d in group:
            n, mine = (ny, y) if which == 0 else (nz, z)
            chunk = wrap(mine + d, n)
            value = flat(sa[chunk] if which == 0 else sb[chunk])
            pieces += halves(value)
            rows_of.append((which, chunk, value.shape[0]))
        made = jnp.dot(jnp.concatenate(pieces, axis=0), b2[...], preferred_element_type=jnp.float32)
        made = made[:, :wide] + made[:, wide:]
        at_row = 0
        for which, chunk, high in rows_of:
            part = (made[at_row : at_row + high] + made[at_row + high : at_row + 2 * high]) * inverse
            at_row += 2 * high
            for k, e in enumerate(orders[which]):
                if which == 0:
                    block, zz = chunk, wrap(z + nz - e, nz)
                else:
                    block, zz = wrap(y + ny - e, ny), chunk
                unit = first + block * wide + which * half_wide + zz * 8 + line8
                ob[block, which, zz] = part[k * 8 : (k + 1) * 8] + jnp.where(unit == col, weight, 0.0)

    work = [(1, 0), (0, 0)]
    for d in range(1, max(ny, nz) // 2):
        for which in (1, 0):
            if d < extent[which] // 2:
                work += [(which, d), (which, extent[which] - d)]

    top = max(ny, nz) // 2
    done = 0
    for d in range(1, top + 1):
        for k in range(subs):
            for which in (0, 1):
                if d <= extent[which] // 2:
                    take(which, d, k)
            for now, act in PLAN:
                if now == (d, k):
                    act_of[act]()
            able = [w for w in work[done:] if min(w[1], extent[w[0]] - w[1]) < d]
            if now_ready[0] and able:
                emit(able[:GROUP])
                done += len(able[:GROUP])
    if not now_ready[0]:
        act_of["ready"]()
    while done < len(work):
        emit(work[done : done + GROUP])
        done += GROUP
    emit([(which, extent[which] // 2) for which in (1, 0)])

    for k in range(ny):
        turned = ob[k].reshape(wide, wide).T
        left, right = turned[:half_wide], turned[half_wide:]
        lanes = pl.ds(pl.multiple_of((c * ny + k) * wide, wide), wide)
        st[k] = jnp.where(c == 0, right, left)
        send(st.at[k], out.at[:, lanes], s_out, r_out, at(z, y, mate, q))
        out[:, lanes] = jnp.where(c == 0, left, right)
    for which, n, raw, red, buf in ((0, nz, ra, qa, sa), (1, ny, rb, qb, sb)):
        sent(raw.at[pl.ds(0, n - 1)], s_raw.at[which, 0])
        sent(raw.at[0, 0], s_raw.at[which, 1])
        sent(red.at[pl.ds(0, red.shape[0] - 1)], s_red.at[which])
        sent(buf.at[0, pl.ds(0, n - 1)], s_ag.at[which])
        sent(buf.at[pl.ds(0, buf.shape[0] - 1)], s_ring.at[which])
    sent(sm1.at[pl.ds(0, nz - 1), 0], s_sm1.at[1])

    @pl.when(c == 0)
    def _():
        sent(sm1.at[0, 0], s_sm1.at[0])

    @pl.when(c == 1)
    def _():
        for cc in (0, 1):
            sent(sm2.at[pl.ds(0, ny - 1)], s_sm2.at[1 + cc])
        sent(sm2.at[0], s_sm2.at[0])

    @pl.when(hop != 0)
    def _():
        sent(sb.at[z, 0], s_op)

    @pl.when((c == root_c) & (away == 0))
    def _():
        for h in (0, 1):
            for d in beside:
                sent(bo.at[h], s_x.at[h, d])

    if nx > 2:

        @pl.when((c == root_c) & (wrap(away, 2) == 1))
        def _():
            for h in (0, 1):
                sent(bo.at[h, pl.ds(0, mid)], s_x.at[h, 2])

    @pl.when(c == root_c)
    def _():
        for h in (0, 1):
            sent(bo.at[h], s_sib.at[h])

    sent(st, s_out)
    arrived(out.at[:, pl.ds(pl.multiple_of(mate * (ny * wide), wide), ny * wide)], r_out)


def body(hidden_panel, row_signs, sample_rows, sample_counts, ridge_weight):
    nx = lax.axis_size("cols")
    nz = 2 * nx
    ny = lax.axis_size("rows") // (2 * nz)
    width, length = hidden_panel.shape
    shards = sample_counts.shape[0]
    cap = -(-shards * sample_rows.shape[1] // 128) * 128
    half_wide = 8 * nz
    dma, f32, i32, bf16 = pltpu.SemaphoreType.DMA, jnp.float32, jnp.int32, jnp.bfloat16
    m = max(nz, ny)
    vmem = pl.BlockSpec(memory_space=pltpu.VMEM)
    smem = pl.BlockSpec(memory_space=pltpu.SMEM)
    hbm = pl.BlockSpec(memory_space=pl.ANY)
    result = pl.pallas_call(
        functools.partial(kernel, nz, ny, nx, cap),
        out_shape=pltpu.VMEM((half_wide, width), f32),
        in_specs=[hbm, vmem, smem, vmem, smem],
        out_specs=vmem,
        scratch_shapes=[
            pltpu.VMEM((2, ny, 2, nz, 8, length), f32),
            pltpu.VMEM((nz, 2, ny, 8, length), f32),
            pltpu.VMEM((ny, 2, nz, 8, length), f32),
            pltpu.VMEM((nz, 2, 1, cap), i32),
            pltpu.VMEM((ny, 1, cap), i32),
            pltpu.VMEM((ny, 8, cap), f32),
            pltpu.VMEM((nz, 8, cap), f32),
            pltpu.VMEM((ny, 8, cap), f32),
            pltpu.VMEM((nz, 8, cap), f32),
            pltpu.VMEM((ny, nz, 8, cap), f32),
            pltpu.VMEM((nz, ny, 8, cap), f32),
            pltpu.VMEM((2, nz, 8, cap), f32),
            pltpu.VMEM((nz, 8, cap), f32),
            pltpu.VMEM((cap, 4 * half_wide), bf16),
            pltpu.VMEM((2 * length, cap), bf16),
            pltpu.VMEM((ny, 2, nz, 8, 2 * half_wide), f32),
            pltpu.VMEM((ny, half_wide, 2 * half_wide), f32),
            dma(()),
            dma((2, 2)),
            dma((2, m)),
            dma((2,)),
            dma((2,)),
            dma((3,)),
            dma((2,)),
            dma((2,)),
            dma((2,)),
            dma((2,)),
            dma((2, m)),
            dma(()),
            dma(()),
            dma((2, nx)),
            dma((2, nx)),
            dma((2,)),
            dma((2,)),
            dma((2,)),
            dma((2, 2, m // 2, m)),
            dma(()),
            dma(()),
        ],
        compiler_params=pltpu.CompilerParams(collective_id=0, has_side_effects=True),
        name="sketch_gram",
    )(
        hidden_panel.reshape(2, ny, 2, nz, 8, length),
        row_signs.reshape(1, length),
        sample_rows,
        sample_counts.reshape(1, shards),
        ridge_weight.reshape(1, 1),
    )
    return result.T


def solution(mesh):
    placed = (P("cols", "rows"), P("rows"), P("rows", None), P(), P())
    return jax.shard_map(
        body, mesh=mesh, in_specs=placed, out_specs=P("cols", "rows"), check_vma=False
    )
```

```python
import functools
import math

import jax
import jax.numpy as jnp
from jax import lax
from jax.experimental import pallas as pl
from jax.experimental.pallas import tpu as pltpu
from jax.sharding import PartitionSpec as P

MESH = pl.DeviceIdType.MESH


def halves(value):
    high = value.astype(jnp.bfloat16)
    return high, (value - high.astype(jnp.float32)).astype(jnp.bfloat16)


def wrap(value, n):
    return value & (n - 1) if n & (n - 1) == 0 else lax.rem(value, n)


def signs_of(common):
    for shift in (8, 4, 2, 1):
        common = common ^ (common >> shift)
    return (1 - 2 * (common & 1)).astype(jnp.float32)


def far_first(n):
    return [n // 2] + [d for k in range(n // 2 - 1, 0, -1) for d in (k, n - k)]


def near_first(n):
    return [d for k in range(1, n // 2) for d in (k, n - k)] + [n // 2]


SUBS = 4
GROUP = 4
PLAN = (((1, 2), "relay0"), ((1, 3), "relay1"), ((2, 0), "far0"), ((2, 2), "far1"), ((2, 3), "ready"))


def kernel(
    nz, ny, nx, cap, panel, signs, rows, counts, ridge, out,
    xs, ra, rb, sm1, sm2, pa, pb, qa, qb, sa, sb, bo, bn, b2, hh, ob, st,
    in_sem, s_raw, r_raw, s_sm1, r_sm1, s_sm2, r_sm2, s_red, r_red, s_ag, r_ag,
    s_op, r_op, s_x, r_x, s_sib, r_sib, s_ring, r_ring, s_out, r_out,
):
    length = panel.shape[-1]
    shards = counts.shape[1]
    me = lax.axis_index("rows")
    q = lax.axis_index("cols")
    c = wrap(me, 2)
    y = wrap(me >> 1, ny)
    z = (me >> 1) // ny if ny & (ny - 1) else me >> ny.bit_length()
    mate = 1 - c

    def at(zz, yy, cc, xx):
        return ((zz * ny + yy) * 2 + cc, xx)

    def up_z(d):
        return wrap(z + d, nz)

    def up_y(d):
        return wrap(y + d, ny)

    def send(src, dst, ss, rs, to):
        pltpu.make_async_remote_copy(
            src_ref=src, dst_ref=dst, send_sem=ss, recv_sem=rs, device_id=to, device_id_type=MESH
        ).start()

    def arrived(slot, sem):
        pltpu.make_async_copy(slot, slot, sem).wait()

    def sent(src, sem):
        pltpu.make_async_copy(src, src, sem).wait()

    load = pltpu.make_async_copy(panel, xs, in_sem)
    load.start()

    barrier = pltpu.get_barrier_semaphore()
    greeted = [at(z, y, mate, q)]
    for d in range(1, nz):
        greeted += [at(up_z(d), y, cc, q) for cc in (0, 1)]
    for d in range(1, ny):
        greeted += [at(z, up_y(d), cc, q) for cc in (0, 1)]
    for d in range(1, nx):
        greeted.append(at(z, y, c, wrap(q + d, nx)))
    for to in greeted:
        pl.semaphore_signal(barrier, inc=1, device_id=to, device_id_type=MESH)

    count_row = counts[...].astype(jnp.float32)
    lane = lax.broadcasted_iota(jnp.int32, (shards, shards), 1)
    line = lax.broadcasted_iota(jnp.int32, (shards, shards), 0)
    ends = jnp.sum(jnp.where(lane <= line, count_row, 0.0), axis=1, keepdims=True)
    slot = lax.broadcasted_iota(jnp.int32, (1, cap), 1)
    passed = ends <= slot.astype(jnp.float32)
    pk = jnp.sum(passed.astype(jnp.float32), axis=0, keepdims=True).astype(jnp.int32)
    block = lax.broadcasted_iota(jnp.int32, (1, shards), 1)
    before = jnp.sum(jnp.where(block < me, count_row, 0.0), axis=1, keepdims=True)
    total = jnp.sum(count_row, axis=1, keepdims=True)
    place = slot - before.astype(jnp.int32)
    own = jnp.zeros((1, cap), jnp.int32)
    for j in range(rows.shape[1]):
        own = jnp.where((pk == me) & (place == j), rows[0, j] - me * length, own)
    sm1[z, c] = own

    load.wait()
    xs[...] = xs[...] * signs[...]
    pl.semaphore_wait(barrier, len(greeted))

    @pl.when(c == 0)
    def _():
        send(sm1.at[z, 0], sm1.at[z, 0], s_sm1.at[0], r_sm1.at[0], at(z, y, 1, q))

    for d in range(1, nz):
        send(sm1.at[z, c], sm1.at[z, c], s_sm1.at[1], r_sm1.at[1], at(up_z(d), y, 1, q))

    def raw_z(d):
        for cc in (0, 1):
            send(xs.at[cc, :, 0, up_z(d)], ra.at[z, c], s_raw.at[0, 0], r_raw.at[0, d], at(up_z(d), y, cc, q))

    def raw_y(d):
        for cc in (0, 1):
            send(xs.at[cc, up_y(d), 1], rb.at[y, c], s_raw.at[1, 0], r_raw.at[1, d], at(z, up_y(d), cc, q))

    send(xs.at[mate, :, 0, z], ra.at[z, c], s_raw.at[0, 1], r_raw.at[0, 0], at(z, y, mate, q))
    send(xs.at[mate, y, 1], rb.at[y, c], s_raw.at[1, 1], r_raw.at[1, 0], at(z, y, mate, q))

    order_z, order_y = near_first(nz), near_first(ny)

    @pl.when(c == 0)
    def _():
        for k in range(max(len(order_z), len(order_y))):
            if k < len(order_z):
                raw_z(order_z[k])
            if k < len(order_y):
                raw_y(order_y[k])

    @pl.when(c == 1)
    def _():
        for d in order_z:
            raw_z(d)
        arrived(sm1.at[z, 0], r_sm1.at[0])
        arrived(sm1.at[pl.ds(0, nz - 1)], r_sm1.at[1])
        sm2[y] = jnp.sum(sm1[...].reshape(2 * nz, 1, cap), axis=0)
        for d in range(1, ny):
            for cc in (0, 1):
                send(sm2.at[y], sm2.at[y], s_sm2.at[1 + cc], r_sm2.at[1], at(z, up_y(d), cc, q))
        send(sm2.at[y], sm2.at[y], s_sm2.at[0], r_sm2.at[0], at(z, y, 0, q))
        for d in order_y:
            raw_y(d)

    @pl.when(c == 0)
    def _():
        arrived(sm2.at[y], r_sm2.at[0])

    arrived(sm2.at[pl.ds(0, ny - 1)], r_sm2.at[1])
    local_row = jnp.sum(sm2[...], axis=0)

    token = lax.broadcasted_iota(jnp.int32, (length, cap), 0)
    scale = 1.0 / math.sqrt(length * shards)
    live = jnp.where(slot.astype(jnp.float32) < total, scale, 0.0)
    sign = (signs_of(token & local_row) * live).astype(jnp.bfloat16)
    hh[:length] = sign
    hh[length:] = sign

    def share(parts, acc):
        pieces = [jnp.concatenate(halves(value), axis=1) for value, _ in parts]
        made = jnp.dot(jnp.concatenate(pieces, axis=0), hh[...], preferred_element_type=jnp.float32)
        high = made.shape[0] // len(parts)
        for k, (_, source) in enumerate(parts):
            term = made[k * high : (k + 1) * high] * signs_of(pk & source)
            acc = term if acc is None else acc + term
        return acc

    def batches(n):
        return [(0,)] + [(d, n - d) for d in range(1, n // 2)] + [(n // 2,)]

    def flat(value):
        return value.reshape(-1, value.shape[-1])

    def block_of(zz, yy, cc):
        return (zz * ny + yy) * 2 + cc

    def share_of(which, batch, acc):
        n, mine, buf = (nz, z, ra) if which == 0 else (ny, y, rb)
        parts = []
        for d in batch:
            far = wrap(mine + n - d, n) if d else mine
            for cc in (0, 1):
                if d == 0 and cc == 0:
                    held = xs[c, :, 0, z] if which == 0 else xs[c, y, 1]
                    parts.append((flat(held), block_of(z, y, c)))
                    continue
                source = mate if d == 0 else cc
                if cc == 0:
                    arrived(buf.at[far], r_raw.at[which, d])
                elif d == 0:
                    arrived(buf.at[far, source], r_raw.at[which, 0])
                block_at = block_of(far, y, source) if which == 0 else block_of(z, far, source)
                parts.append((flat(buf[far, source]), block_at))
        return share(parts, acc)

    steps_z, steps_y = batches(nz), batches(ny)
    acc_z = acc_y = None
    for k in range(max(len(steps_z), len(steps_y))):
        if k < len(steps_z):
            acc_z = share_of(0, steps_z[k], acc_z)
            if k == len(steps_z) - 1:
                pa[...] = acc_z.reshape(ny, 8, cap)
                for d in far_first(ny):
                    send(pa.at[up_y(d)], qa.at[y], s_red.at[0], r_red.at[0], at(z, up_y(d), c, q))
        if k < len(steps_y):
            acc_y = share_of(1, steps_y[k], acc_y)
            if k == len(steps_y) - 1:
                pb[...] = acc_y.reshape(nz, 8, cap)
                for d in far_first(nz):
                    send(pb.at[up_z(d)], qb.at[z], s_red.at[1], r_red.at[1], at(up_z(d), y, c, q))

    subs = min(SUBS, nz, ny)

    def hold(which, d, k):
        n, mine, buf = (ny, y, sa) if which == 0 else (nz, z, sb)
        size = buf.shape[1] // subs
        return buf.at[wrap(mine + d, n), pl.ds(k * size, size)]

    extent = (ny, nz)
    orders = ([0] + near_first(nz), [0] + near_first(ny))

    def come_from(which, way, d):
        return (extent[which] - d) % extent[which] if way == 0 else d

    def passes(which, way, d, k):
        n = extent[which]
        return d < n // 2 or (d == n // 2 and k % 2 == way)

    def pass_on(which, d, k, ways=(0, 1)):
        n = extent[which]
        leap = min(2, n // 2)
        for way in ways:
            view = hold(which, come_from(which, way, d), k)
            for far in ([d + 1] if d + 1 < n // 2 else []) + ([n // 2] if d == n // 2 - leap else []):
                if not passes(which, way, far, k):
                    continue
                step = far - d if way == 0 else n - (far - d)
                to = at(z, up_y(step), c, q) if which == 0 else at(up_z(step), y, c, q)
                send(view, view, s_ring.at[which], r_ring.at[which, way, far - 1, k], to)

    def take(which, d, k):
        for way in (0, 1):
            if passes(which, way, d, k):
                view = hold(which, come_from(which, way, d), k)
                arrived(view, r_ring.at[which, way, d - 1, k])
                pass_on(which, d, k, (way,))

    target = 2 * q + c
    hop = wrap(target - z + nz, nz)

    piece = pa[y]
    arrived(qa.at[pl.ds(0, ny - 1)], r_red.at[0])
    for d in range(1, ny):
        piece = piece + qa[up_y(ny - d)]
    sa[y, 0] = piece
    for d in near_first(nz):
        send(sa.at[y, 0], sa.at[y, orders[0].index(d)], s_ag.at[0], r_ag.at[0, orders[0].index(d) * subs // nz], at(up_z(d), y, c, q))
    piece = pb[z]
    arrived(qb.at[pl.ds(0, nz - 1)], r_red.at[1])
    for d in range(1, nz):
        piece = piece + qb[up_z(nz - d)]
    sb[z, 0] = piece

    @pl.when(hop != 0)
    def _():
        send(sb.at[z, 0], bo.at[1, z], s_op, r_op, at(target, y, c, q))

    @pl.when(hop == 0)
    def _():
        bo[1, z] = piece

    for d in near_first(ny):
        send(sb.at[z, 0], sb.at[z, orders[1].index(d)], s_ag.at[1], r_ag.at[1, orders[1].index(d) * subs // ny], at(z, up_y(d), c, q))
    for k in range(subs):
        for which in (0, 1):
            mine, buf = (y, sa) if which == 0 else (z, sb)
            size = buf.shape[1] // subs
            begin = max(k * size, 1)
            if begin < (k + 1) * size:
                arrived(buf.at[mine, pl.ds(begin, (k + 1) * size - begin)], r_ag.at[which, k])
            pass_on(which, 0, k)

    root_c = wrap(z, 2)
    root_q = z >> 1
    away = wrap(q - root_q + nx, nx)
    beside = [d for d in (1, nx - 1) if d] if nx > 2 else [1]
    mid = nz // 2

    @pl.when((c == root_c) & (away == 0))
    def _():
        for d in beside:
            send(sa.at[y], bo.at[0], s_x.at[0, d], r_x.at[0, 0], at(z, y, c, wrap(q + d, nx)))
        send(sa.at[y], bo.at[0], s_sib.at[0], r_sib.at[0], at(z, y, mate, q))
        arrived(bo.at[1, pl.ds(0, nz - 1)], r_op)
        for d in beside:
            send(bo.at[1], bo.at[1], s_x.at[1, d], r_x.at[1, 0], at(z, y, c, wrap(q + d, nx)))
        send(bo.at[1], bo.at[1], s_sib.at[1], r_sib.at[1], at(z, y, mate, q))
        bo[0] = sa[y]

    def relay(h):
        for d in beside:
            part = pl.ds(0 if d == 1 else mid, mid)

            @pl.when((c == root_c) & (away == d))
            def _():
                arrived(bo.at[h], r_x.at[h, 0])
                if nx > 2:
                    there = wrap(root_q + 2, nx)
                    view = bo.at[h, part]
                    send(view, view, s_x.at[h, 2], r_x.at[h, d], at(z, y, c, there))
                send(bo.at[h], bo.at[h], s_sib.at[h], r_sib.at[h], at(z, y, mate, q))

    def relay_far(h):
        if nx > 2:

            @pl.when((c == root_c) & (away == 2))
            def _():
                for d in beside:
                    view = bo.at[h, pl.ds(0 if d == 1 else mid, mid)]
                    arrived(view, r_x.at[h, d])
                send(bo.at[h], bo.at[h], s_sib.at[h], r_sib.at[h], at(z, y, mate, q))

    wide = 2 * nz * 8
    half_wide = wide // 2

    now_ready = [False]

    def columns_ready():
        @pl.when(c != root_c)
        def _():
            for h in (0, 1):
                arrived(bo.at[h], r_sib.at[h])

        for k, e in enumerate(orders[0]):
            bn[wrap(z + nz - e, nz)] = bo[0, k]
        b_high, b_low = halves(jnp.concatenate([flat(bn[...]), flat(bo[1])], axis=0))
        b2[:, :wide] = b_high.T
        b2[:, wide:] = b_low.T

    def ready_now():
        columns_ready()
        now_ready[0] = True

    def tail_relays():
        for name in ("relay0", "relay1", "far0", "far1"):
            if name not in acted:
                act_of[name]()
        ready_now()

    acted = set()

    def once(name, act):
        def run():
            if name not in acted:
                acted.add(name)
                act()

        return run

    act_of = {
        "relay0": once("relay0", lambda: relay(0)),
        "relay1": once("relay1", lambda: relay(1)),
        "far0": once("far0", lambda: relay_far(0)),
        "far1": once("far1", lambda: relay_far(1)),
        "ready": once("ready", tail_relays),
    }

    units = 2 * ny * wide
    first = q * units + c * (ny * wide)
    col = (z * ny + y) * wide + lax.broadcasted_iota(jnp.int32, (1, wide), 1)
    inverse = 1.0 / total
    weight = ridge[0, 0]
    line8 = lax.broadcasted_iota(jnp.int32, (8, 1), 0)

    def emit(group):
        pieces, rows_of = [], []
        for which, d in group:
            n, mine = (ny, y) if which == 0 else (nz, z)
            chunk = wrap(mine + d, n)
            value = flat(sa[chunk] if which == 0 else sb[chunk])
            pieces += halves(value)
            rows_of.append((which, chunk, value.shape[0]))
        made = jnp.dot(jnp.concatenate(pieces, axis=0), b2[...], preferred_element_type=jnp.float32)
        made = made[:, :wide] + made[:, wide:]
        at_row = 0
        for which, chunk, high in rows_of:
            part = (made[at_row : at_row + high] + made[at_row + high : at_row + 2 * high]) * inverse
            at_row += 2 * high
            for k, e in enumerate(orders[which]):
                if which == 0:
                    block, zz = chunk, wrap(z + nz - e, nz)
                else:
                    block, zz = wrap(y + ny - e, ny), chunk
                unit = first + block * wide + which * half_wide + zz * 8 + line8
                ob[block, which, zz] = part[k * 8 : (k + 1) * 8] + jnp.where(unit == col, weight, 0.0)

    work = [(1, 0), (0, 0)]
    for d in range(1, max(ny, nz) // 2):
        for which in (1, 0):
            if d < extent[which] // 2:
                work += [(which, d), (which, extent[which] - d)]

    top = max(ny, nz) // 2
    done = 0
    for d in range(1, top + 1):
        for k in range(subs):
            for which in (0, 1):
                if d <= extent[which] // 2:
                    take(which, d, k)
            for now, act in PLAN:
                if now == (d, k):
                    act_of[act]()
            able = [w for w in work[done:] if min(w[1], extent[w[0]] - w[1]) < d]
            if now_ready[0] and able:
                emit(able[:GROUP])
                done += len(able[:GROUP])
    if not now_ready[0]:
        act_of["ready"]()
    while done < len(work):
        emit(work[done : done + GROUP])
        done += GROUP
    emit([(which, extent[which] // 2) for which in (1, 0)])

    for k in range(ny):
        turned = ob[k].reshape(wide, wide).T
        left, right = turned[:half_wide], turned[half_wide:]
        lanes = pl.ds(pl.multiple_of((c * ny + k) * wide, wide), wide)
        st[k] = jnp.where(c == 0, right, left)
        send(st.at[k], out.at[:, lanes], s_out, r_out, at(z, y, mate, q))
        out[:, lanes] = jnp.where(c == 0, left, right)
    for which, n, raw, red, buf in ((0, nz, ra, qa, sa), (1, ny, rb, qb, sb)):
        sent(raw.at[pl.ds(0, n - 1)], s_raw.at[which, 0])
        sent(raw.at[0, 0], s_raw.at[which, 1])
        sent(red.at[pl.ds(0, red.shape[0] - 1)], s_red.at[which])
        sent(buf.at[0, pl.ds(0, n - 1)], s_ag.at[which])
        sent(buf.at[pl.ds(0, buf.shape[0] - 1)], s_ring.at[which])
    sent(sm1.at[pl.ds(0, nz - 1), 0], s_sm1.at[1])

    @pl.when(c == 0)
    def _():
        sent(sm1.at[0, 0], s_sm1.at[0])

    @pl.when(c == 1)
    def _():
        for cc in (0, 1):
            sent(sm2.at[pl.ds(0, ny - 1)], s_sm2.at[1 + cc])
        sent(sm2.at[0], s_sm2.at[0])

    @pl.when(hop != 0)
    def _():
        sent(sb.at[z, 0], s_op)

    @pl.when((c == root_c) & (away == 0))
    def _():
        for h in (0, 1):
            for d in beside:
                sent(bo.at[h], s_x.at[h, d])

    if nx > 2:

        @pl.when((c == root_c) & (wrap(away, 2) == 1))
        def _():
            for h in (0, 1):
                sent(bo.at[h, pl.ds(0, mid)], s_x.at[h, 2])

    @pl.when(c == root_c)
    def _():
        for h in (0, 1):
            sent(bo.at[h], s_sib.at[h])

    sent(st, s_out)
    arrived(out.at[:, pl.ds(pl.multiple_of(mate * (ny * wide), wide), ny * wide)], r_out)


def body(hidden_panel, row_signs, sample_rows, sample_counts, ridge_weight):
    nx = lax.axis_size("cols")
    nz = 2 * nx
    ny = lax.axis_size("rows") // (2 * nz)
    width, length = hidden_panel.shape
    shards = sample_counts.shape[0]
    full = -(-shards * sample_rows.shape[1] // 128) * 128
    half_wide = 8 * nz
    dma, f32, i32, bf16 = pltpu.SemaphoreType.DMA, jnp.float32, jnp.int32, jnp.bfloat16
    m = max(nz, ny)
    vmem = pl.BlockSpec(memory_space=pltpu.VMEM)
    smem = pl.BlockSpec(memory_space=pltpu.SMEM)
    hbm = pl.BlockSpec(memory_space=pl.ANY)
    def run(cap, number):
        return pl.pallas_call(
            functools.partial(kernel, nz, ny, nx, cap),
            out_shape=pltpu.VMEM((half_wide, width), f32),
            in_specs=[hbm, vmem, smem, vmem, smem],
            out_specs=vmem,
            scratch_shapes=[
                pltpu.VMEM((2, ny, 2, nz, 8, length), f32),
                pltpu.VMEM((nz, 2, ny, 8, length), f32),
                pltpu.VMEM((ny, 2, nz, 8, length), f32),
                pltpu.VMEM((nz, 2, 1, cap), i32),
                pltpu.VMEM((ny, 1, cap), i32),
                pltpu.VMEM((ny, 8, cap), f32),
                pltpu.VMEM((nz, 8, cap), f32),
                pltpu.VMEM((ny, 8, cap), f32),
                pltpu.VMEM((nz, 8, cap), f32),
                pltpu.VMEM((ny, nz, 8, cap), f32),
                pltpu.VMEM((nz, ny, 8, cap), f32),
                pltpu.VMEM((2, nz, 8, cap), f32),
                pltpu.VMEM((nz, 8, cap), f32),
                pltpu.VMEM((cap, 4 * half_wide), bf16),
                pltpu.VMEM((2 * length, cap), bf16),
                pltpu.VMEM((ny, 2, nz, 8, 2 * half_wide), f32),
                pltpu.VMEM((ny, half_wide, 2 * half_wide), f32),
                dma(()),
                dma((2, 2)),
                dma((2, m)),
                dma((2,)),
                dma((2,)),
                dma((3,)),
                dma((2,)),
                dma((2,)),
                dma((2,)),
                dma((2,)),
                dma((2, m)),
                dma(()),
                dma(()),
                dma((2, nx)),
                dma((2, nx)),
                dma((2,)),
                dma((2,)),
                dma((2,)),
                dma((2, 2, m // 2, m)),
                dma(()),
                dma(()),
            ],
            compiler_params=pltpu.CompilerParams(collective_id=number, has_side_effects=True),
            name="sketch_gram",
        )(
            hidden_panel.reshape(2, ny, 2, nz, 8, length),
            row_signs.reshape(1, length),
            sample_rows,
            sample_counts.reshape(1, shards),
            ridge_weight.reshape(1, 1),
        )

    small = full * 3 // 512 * 128
    if small == 0:
        return run(full, 0).T
    result = lax.cond(jnp.sum(sample_counts) <= small, lambda: run(small, 1), lambda: run(full, 0))
    return result.T


def solution(mesh):
    placed = (P("cols", "rows"), P("rows"), P("rows", None), P(), P())
    return jax.shard_map(
        body, mesh=mesh, in_specs=placed, out_specs=P("cols", "rows"), check_vma=False
    )
```

```python
import functools
import math

import jax
import jax.numpy as jnp
from jax import lax
from jax.experimental import pallas as pl
from jax.experimental.pallas import tpu as pltpu
from jax.sharding import PartitionSpec as P

MESH = pl.DeviceIdType.MESH


def halves(value):
    high = value.astype(jnp.bfloat16)
    return high, (value - high.astype(jnp.float32)).astype(jnp.bfloat16)


def wrap(value, n):
    return value & (n - 1) if n & (n - 1) == 0 else lax.rem(value, n)


def signs_of(common):
    for shift in (8, 4, 2, 1):
        common = common ^ (common >> shift)
    return (1 - 2 * (common & 1)).astype(jnp.float32)


def far_first(n):
    return [n // 2] + [d for k in range(n // 2 - 1, 0, -1) for d in (k, n - k)]


def near_first(n):
    return [d for k in range(1, n // 2) for d in (k, n - k)] + [n // 2]


SUBS = 4
GROUP = 4
PLAN = (((1, 2), "relay0"), ((1, 3), "relay1"), ((2, 0), "far0"), ((2, 2), "far1"), ((2, 3), "ready"))


def kernel(
    nz, ny, nx, cap, panel, signs, rows, counts, ridge, out,
    xs, ra, rb, sm1, sm2, pa, pb, qa, qb, sa, sb, bo, bn, b2, hh, ob, st,
    in_sem, s_raw, r_raw, s_sm1, r_sm1, s_sm2, r_sm2, s_red, r_red, s_ag, r_ag,
    s_op, r_op, s_x, r_x, s_sib, r_sib, s_ring, r_ring, s_out, r_out,
):
    length = panel.shape[-1]
    shards = counts.shape[1]
    me = lax.axis_index("rows")
    q = lax.axis_index("cols")
    c = wrap(me, 2)
    y = wrap(me >> 1, ny)
    z = (me >> 1) // ny if ny & (ny - 1) else me >> ny.bit_length()
    mate = 1 - c

    def at(zz, yy, cc, xx):
        return ((zz * ny + yy) * 2 + cc, xx)

    def up_z(d):
        return wrap(z + d, nz)

    def up_y(d):
        return wrap(y + d, ny)

    def send(src, dst, ss, rs, to):
        pltpu.make_async_remote_copy(
            src_ref=src, dst_ref=dst, send_sem=ss, recv_sem=rs, device_id=to, device_id_type=MESH
        ).start()

    def arrived(slot, sem):
        pltpu.make_async_copy(slot, slot, sem).wait()

    def sent(src, sem):
        pltpu.make_async_copy(src, src, sem).wait()

    load = pltpu.make_async_copy(panel, xs, in_sem)
    load.start()

    barrier = pltpu.get_barrier_semaphore()
    greeted = [at(z, y, mate, q)]
    for d in range(1, nz):
        greeted += [at(up_z(d), y, cc, q) for cc in (0, 1)]
    for d in range(1, ny):
        greeted += [at(z, up_y(d), cc, q) for cc in (0, 1)]
    for d in range(1, nx):
        greeted.append(at(z, y, c, wrap(q + d, nx)))
    for to in greeted:
        pl.semaphore_signal(barrier, inc=1, device_id=to, device_id_type=MESH)

    count_row = counts[...].astype(jnp.float32)
    lane = lax.broadcasted_iota(jnp.int32, (shards, shards), 1)
    line = lax.broadcasted_iota(jnp.int32, (shards, shards), 0)
    ends = jnp.sum(jnp.where(lane <= line, count_row, 0.0), axis=1, keepdims=True)
    slot = lax.broadcasted_iota(jnp.int32, (1, cap), 1)
    passed = ends <= slot.astype(jnp.float32)
    pk = jnp.sum(passed.astype(jnp.float32), axis=0, keepdims=True).astype(jnp.int32)
    block = lax.broadcasted_iota(jnp.int32, (1, shards), 1)
    before = jnp.sum(jnp.where(block < me, count_row, 0.0), axis=1, keepdims=True)
    total = jnp.sum(count_row, axis=1, keepdims=True)
    place = slot - before.astype(jnp.int32)
    own = jnp.zeros((1, cap), jnp.int32)
    for j in range(rows.shape[1]):
        own = jnp.where((pk == me) & (place == j), rows[0, j] - me * length, own)
    sm1[z, c] = own

    load.wait()
    xs[...] = xs[...] * signs[...]
    pl.semaphore_wait(barrier, len(greeted))

    @pl.when(c == 0)
    def _():
        send(sm1.at[z, 0], sm1.at[z, 0], s_sm1.at[0], r_sm1.at[0], at(z, y, 1, q))

    for d in range(1, nz):
        send(sm1.at[z, c], sm1.at[z, c], s_sm1.at[1], r_sm1.at[1], at(up_z(d), y, 1, q))

    def raw_z(d):
        for cc in (0, 1):
            send(xs.at[cc, :, 0, up_z(d)], ra.at[z, c], s_raw.at[0, 0], r_raw.at[0, d], at(up_z(d), y, cc, q))

    def raw_y(d):
        for cc in (0, 1):
            send(xs.at[cc, up_y(d), 1], rb.at[y, c], s_raw.at[1, 0], r_raw.at[1, d], at(z, up_y(d), cc, q))

    send(xs.at[mate, :, 0, z], ra.at[z, c], s_raw.at[0, 1], r_raw.at[0, 0], at(z, y, mate, q))
    send(xs.at[mate, y, 1], rb.at[y, c], s_raw.at[1, 1], r_raw.at[1, 0], at(z, y, mate, q))

    order_z, order_y = near_first(nz), near_first(ny)

    @pl.when(c == 0)
    def _():
        for k in range(max(len(order_z), len(order_y))):
            if k < len(order_z):
                raw_z(order_z[k])
            if k < len(order_y):
                raw_y(order_y[k])

    @pl.when(c == 1)
    def _():
        for d in order_z:
            raw_z(d)
        arrived(sm1.at[z, 0], r_sm1.at[0])
        arrived(sm1.at[pl.ds(0, nz - 1)], r_sm1.at[1])
        sm2[y] = jnp.sum(sm1[...].reshape(2 * nz, 1, cap), axis=0)
        for d in range(1, ny):
            for cc in (0, 1):
                send(sm2.at[y], sm2.at[y], s_sm2.at[1 + cc], r_sm2.at[1], at(z, up_y(d), cc, q))
        send(sm2.at[y], sm2.at[y], s_sm2.at[0], r_sm2.at[0], at(z, y, 0, q))
        for d in order_y:
            raw_y(d)

    @pl.when(c == 0)
    def _():
        arrived(sm2.at[y], r_sm2.at[0])

    arrived(sm2.at[pl.ds(0, ny - 1)], r_sm2.at[1])
    local_row = jnp.sum(sm2[...], axis=0)

    token = lax.broadcasted_iota(jnp.int32, (length, cap), 0)
    scale = 1.0 / math.sqrt(length * shards)
    live = jnp.where(slot.astype(jnp.float32) < total, scale, 0.0)
    sign = (signs_of(token & local_row) * live).astype(jnp.bfloat16)
    hh[:length] = sign
    hh[length:] = sign

    def share(parts, acc):
        pieces = [jnp.concatenate(halves(value), axis=1) for value, _ in parts]
        made = jnp.dot(jnp.concatenate(pieces, axis=0), hh[...], preferred_element_type=jnp.float32)
        high = made.shape[0] // len(parts)
        for k, (_, source) in enumerate(parts):
            term = made[k * high : (k + 1) * high] * signs_of(pk & source)
            acc = term if acc is None else acc + term
        return acc

    def batches(n):
        return [(0,)] + [(d, n - d) for d in range(1, n // 2)] + [(n // 2,)]

    def flat(value):
        return value.reshape(-1, value.shape[-1])

    def block_of(zz, yy, cc):
        return (zz * ny + yy) * 2 + cc

    def share_of(which, batch, acc):
        n, mine, buf = (nz, z, ra) if which == 0 else (ny, y, rb)
        parts = []
        for d in batch:
            far = wrap(mine + n - d, n) if d else mine
            for cc in (0, 1):
                if d == 0 and cc == 0:
                    held = xs[c, :, 0, z] if which == 0 else xs[c, y, 1]
                    parts.append((flat(held), block_of(z, y, c)))
                    continue
                source = mate if d == 0 else cc
                if cc == 0:
                    arrived(buf.at[far], r_raw.at[which, d])
                elif d == 0:
                    arrived(buf.at[far, source], r_raw.at[which, 0])
                block_at = block_of(far, y, source) if which == 0 else block_of(z, far, source)
                parts.append((flat(buf[far, source]), block_at))
        return share(parts, acc)

    steps_z, steps_y = batches(nz), batches(ny)
    acc_z = acc_y = None
    for k in range(max(len(steps_z), len(steps_y))):
        if k < len(steps_z):
            acc_z = share_of(0, steps_z[k], acc_z)
            if k == len(steps_z) - 1:
                pa[...] = acc_z.reshape(ny, 8, cap)
                for d in far_first(ny):
                    send(pa.at[up_y(d)], qa.at[y], s_red.at[0], r_red.at[0], at(z, up_y(d), c, q))
        if k < len(steps_y):
            acc_y = share_of(1, steps_y[k], acc_y)
            if k == len(steps_y) - 1:
                pb[...] = acc_y.reshape(nz, 8, cap)
                for d in far_first(nz):
                    send(pb.at[up_z(d)], qb.at[z], s_red.at[1], r_red.at[1], at(up_z(d), y, c, q))

    subs = min(SUBS, nz, ny)

    def hold(which, d, k):
        n, mine, buf = (ny, y, sa) if which == 0 else (nz, z, sb)
        size = buf.shape[1] // subs
        return buf.at[wrap(mine + d, n), pl.ds(k * size, size)]

    extent = (ny, nz)
    orders = ([0] + near_first(nz), [0] + near_first(ny))

    def come_from(which, way, d):
        return (extent[which] - d) % extent[which] if way == 0 else d

    def passes(which, way, d, k):
        n = extent[which]
        return d < n // 2 or (d == n // 2 and k % 2 == way)

    def pass_on(which, d, k, ways=(0, 1)):
        n = extent[which]
        leap = min(2, n // 2)
        for way in ways:
            view = hold(which, come_from(which, way, d), k)
            for far in ([d + 1] if d + 1 < n // 2 else []) + ([n // 2] if d == n // 2 - leap else []):
                if not passes(which, way, far, k):
                    continue
                step = far - d if way == 0 else n - (far - d)
                to = at(z, up_y(step), c, q) if which == 0 else at(up_z(step), y, c, q)
                send(view, view, s_ring.at[which], r_ring.at[which, way, far - 1, k], to)

    def take(which, d, k):
        for way in (0, 1):
            if passes(which, way, d, k):
                view = hold(which, come_from(which, way, d), k)
                arrived(view, r_ring.at[which, way, d - 1, k])
                pass_on(which, d, k, (way,))

    target = 2 * q + c
    hop = wrap(target - z + nz, nz)

    piece = pa[y]
    arrived(qa.at[pl.ds(0, ny - 1)], r_red.at[0])
    for d in range(1, ny):
        piece = piece + qa[up_y(ny - d)]
    sa[y, 0] = piece
    for d in near_first(nz):
        send(sa.at[y, 0], sa.at[y, orders[0].index(d)], s_ag.at[0], r_ag.at[0, orders[0].index(d) * subs // nz], at(up_z(d), y, c, q))
    piece = pb[z]
    arrived(qb.at[pl.ds(0, nz - 1)], r_red.at[1])
    for d in range(1, nz):
        piece = piece + qb[up_z(nz - d)]
    sb[z, 0] = piece

    @pl.when(hop != 0)
    def _():
        send(sb.at[z, 0], bo.at[1, z], s_op, r_op, at(target, y, c, q))

    @pl.when(hop == 0)
    def _():
        bo[1, z] = piece

    for d in near_first(ny):
        send(sb.at[z, 0], sb.at[z, orders[1].index(d)], s_ag.at[1], r_ag.at[1, orders[1].index(d) * subs // ny], at(z, up_y(d), c, q))
    for k in range(subs):
        for which in (0, 1):
            mine, buf = (y, sa) if which == 0 else (z, sb)
            size = buf.shape[1] // subs
            begin = max(k * size, 1)
            if begin < (k + 1) * size:
                arrived(buf.at[mine, pl.ds(begin, (k + 1) * size - begin)], r_ag.at[which, k])
            pass_on(which, 0, k)

    root_c = wrap(z, 2)
    root_q = z >> 1
    away = wrap(q - root_q + nx, nx)
    beside = [d for d in (1, nx - 1) if d] if nx > 2 else [1]
    mid = nz // 2

    @pl.when((c == root_c) & (away == 0))
    def _():
        for d in beside:
            send(sa.at[y], bo.at[0], s_x.at[0, d], r_x.at[0, 0], at(z, y, c, wrap(q + d, nx)))
        send(sa.at[y], bo.at[0], s_sib.at[0], r_sib.at[0], at(z, y, mate, q))
        arrived(bo.at[1, pl.ds(0, nz - 1)], r_op)
        for d in beside:
            send(bo.at[1], bo.at[1], s_x.at[1, d], r_x.at[1, 0], at(z, y, c, wrap(q + d, nx)))
        send(bo.at[1], bo.at[1], s_sib.at[1], r_sib.at[1], at(z, y, mate, q))
        bo[0] = sa[y]

    def relay(h):
        for d in beside:
            part = pl.ds(0 if d == 1 else mid, mid)

            @pl.when((c == root_c) & (away == d))
            def _():
                arrived(bo.at[h], r_x.at[h, 0])
                if nx > 2:
                    there = wrap(root_q + 2, nx)
                    view = bo.at[h, part]
                    send(view, view, s_x.at[h, 2], r_x.at[h, d], at(z, y, c, there))
                send(bo.at[h], bo.at[h], s_sib.at[h], r_sib.at[h], at(z, y, mate, q))

    def relay_far(h):
        if nx > 2:

            @pl.when((c == root_c) & (away == 2))
            def _():
                for d in beside:
                    view = bo.at[h, pl.ds(0 if d == 1 else mid, mid)]
                    arrived(view, r_x.at[h, d])
                send(bo.at[h], bo.at[h], s_sib.at[h], r_sib.at[h], at(z, y, mate, q))

    wide = 2 * nz * 8
    half_wide = wide // 2

    now_ready = [False]

    def columns_ready():
        @pl.when(c != root_c)
        def _():
            for h in (0, 1):
                arrived(bo.at[h], r_sib.at[h])

        for k, e in enumerate(orders[0]):
            bn[wrap(z + nz - e, nz)] = bo[0, k]
        b_high, b_low = halves(jnp.concatenate([flat(bn[...]), flat(bo[1])], axis=0))
        b2[:, :wide] = b_high.T
        b2[:, wide:] = b_low.T

    def ready_now():
        columns_ready()
        now_ready[0] = True

    def tail_relays():
        for name in ("relay0", "relay1", "far0", "far1"):
            if name not in acted:
                act_of[name]()
        ready_now()

    acted = set()

    def once(name, act):
        def run():
            if name not in acted:
                acted.add(name)
                act()

        return run

    act_of = {
        "relay0": once("relay0", lambda: relay(0)),
        "relay1": once("relay1", lambda: relay(1)),
        "far0": once("far0", lambda: relay_far(0)),
        "far1": once("far1", lambda: relay_far(1)),
        "ready": once("ready", tail_relays),
    }

    units = 2 * ny * wide
    first = q * units + c * (ny * wide)
    col = (z * ny + y) * wide + lax.broadcasted_iota(jnp.int32, (1, wide), 1)
    inverse = 1.0 / total
    weight = ridge[0, 0]
    line8 = lax.broadcasted_iota(jnp.int32, (8, 1), 0)

    def emit(group):
        pieces, rows_of = [], []
        for which, d in group:
            n, mine = (ny, y) if which == 0 else (nz, z)
            chunk = wrap(mine + d, n)
            value = flat(sa[chunk] if which == 0 else sb[chunk])
            pieces += halves(value)
            rows_of.append((which, chunk, value.shape[0]))
        made = jnp.dot(jnp.concatenate(pieces, axis=0), b2[...], preferred_element_type=jnp.float32)
        made = made[:, :wide] + made[:, wide:]
        at_row = 0
        for which, chunk, high in rows_of:
            part = (made[at_row : at_row + high] + made[at_row + high : at_row + 2 * high]) * inverse
            at_row += 2 * high
            for k, e in enumerate(orders[which]):
                if which == 0:
                    block, zz = chunk, wrap(z + nz - e, nz)
                else:
                    block, zz = wrap(y + ny - e, ny), chunk
                unit = first + block * wide + which * half_wide + zz * 8 + line8
                ob[block, which, zz] = part[k * 8 : (k + 1) * 8] + jnp.where(unit == col, weight, 0.0)

    work = [(1, 0), (0, 0)]
    for d in range(1, max(ny, nz) // 2):
        for which in (1, 0):
            if d < extent[which] // 2:
                work += [(which, d), (which, extent[which] - d)]

    top = max(ny, nz) // 2
    done = 0
    for d in range(1, top + 1):
        for k in range(subs):
            for which in (1, 0):
                if d <= extent[which] // 2:
                    take(which, d, k)
            for now, act in PLAN:
                if now == (d, k):
                    act_of[act]()
            able = [w for w in work[done:] if min(w[1], extent[w[0]] - w[1]) < d]
            if now_ready[0] and able:
                emit(able[:GROUP])
                done += len(able[:GROUP])
    if not now_ready[0]:
        act_of["ready"]()
    while done < len(work):
        emit(work[done : done + GROUP])
        done += GROUP
    emit([(which, extent[which] // 2) for which in (1, 0)])

    for k in range(ny):
        turned = ob[k].reshape(wide, wide).T
        left, right = turned[:half_wide], turned[half_wide:]
        lanes = pl.ds(pl.multiple_of((c * ny + k) * wide, wide), wide)
        st[k] = jnp.where(c == 0, right, left)
        send(st.at[k], out.at[:, lanes], s_out, r_out, at(z, y, mate, q))
        out[:, lanes] = jnp.where(c == 0, left, right)
    for which, n, raw, red, buf in ((0, nz, ra, qa, sa), (1, ny, rb, qb, sb)):
        sent(raw.at[pl.ds(0, n - 1)], s_raw.at[which, 0])
        sent(raw.at[0, 0], s_raw.at[which, 1])
        sent(red.at[pl.ds(0, red.shape[0] - 1)], s_red.at[which])
        sent(buf.at[0, pl.ds(0, n - 1)], s_ag.at[which])
        sent(buf.at[pl.ds(0, buf.shape[0] - 1)], s_ring.at[which])
    sent(sm1.at[pl.ds(0, nz - 1), 0], s_sm1.at[1])

    @pl.when(c == 0)
    def _():
        sent(sm1.at[0, 0], s_sm1.at[0])

    @pl.when(c == 1)
    def _():
        for cc in (0, 1):
            sent(sm2.at[pl.ds(0, ny - 1)], s_sm2.at[1 + cc])
        sent(sm2.at[0], s_sm2.at[0])

    @pl.when(hop != 0)
    def _():
        sent(sb.at[z, 0], s_op)

    @pl.when((c == root_c) & (away == 0))
    def _():
        for h in (0, 1):
            for d in beside:
                sent(bo.at[h], s_x.at[h, d])

    if nx > 2:

        @pl.when((c == root_c) & (wrap(away, 2) == 1))
        def _():
            for h in (0, 1):
                sent(bo.at[h, pl.ds(0, mid)], s_x.at[h, 2])

    @pl.when(c == root_c)
    def _():
        for h in (0, 1):
            sent(bo.at[h], s_sib.at[h])

    sent(st, s_out)
    arrived(out.at[:, pl.ds(pl.multiple_of(mate * (ny * wide), wide), ny * wide)], r_out)


def body(hidden_panel, row_signs, sample_rows, sample_counts, ridge_weight):
    nx = lax.axis_size("cols")
    nz = 2 * nx
    ny = lax.axis_size("rows") // (2 * nz)
    width, length = hidden_panel.shape
    shards = sample_counts.shape[0]
    full = -(-shards * sample_rows.shape[1] // 128) * 128
    half_wide = 8 * nz
    dma, f32, i32, bf16 = pltpu.SemaphoreType.DMA, jnp.float32, jnp.int32, jnp.bfloat16
    m = max(nz, ny)
    vmem = pl.BlockSpec(memory_space=pltpu.VMEM)
    smem = pl.BlockSpec(memory_space=pltpu.SMEM)
    hbm = pl.BlockSpec(memory_space=pl.ANY)
    def run(cap, number):
        return pl.pallas_call(
            functools.partial(kernel, nz, ny, nx, cap),
            out_shape=pltpu.VMEM((half_wide, width), f32),
            in_specs=[hbm, vmem, smem, vmem, smem],
            out_specs=vmem,
            scratch_shapes=[
                pltpu.VMEM((2, ny, 2, nz, 8, length), f32),
                pltpu.VMEM((nz, 2, ny, 8, length), f32),
                pltpu.VMEM((ny, 2, nz, 8, length), f32),
                pltpu.VMEM((nz, 2, 1, cap), i32),
                pltpu.VMEM((ny, 1, cap), i32),
                pltpu.VMEM((ny, 8, cap), f32),
                pltpu.VMEM((nz, 8, cap), f32),
                pltpu.VMEM((ny, 8, cap), f32),
                pltpu.VMEM((nz, 8, cap), f32),
                pltpu.VMEM((ny, nz, 8, cap), f32),
                pltpu.VMEM((nz, ny, 8, cap), f32),
                pltpu.VMEM((2, nz, 8, cap), f32),
                pltpu.VMEM((nz, 8, cap), f32),
                pltpu.VMEM((cap, 4 * half_wide), bf16),
                pltpu.VMEM((2 * length, cap), bf16),
                pltpu.VMEM((ny, 2, nz, 8, 2 * half_wide), f32),
                pltpu.VMEM((ny, half_wide, 2 * half_wide), f32),
                dma(()),
                dma((2, 2)),
                dma((2, m)),
                dma((2,)),
                dma((2,)),
                dma((3,)),
                dma((2,)),
                dma((2,)),
                dma((2,)),
                dma((2,)),
                dma((2, m)),
                dma(()),
                dma(()),
                dma((2, nx)),
                dma((2, nx)),
                dma((2,)),
                dma((2,)),
                dma((2,)),
                dma((2, 2, m // 2, m)),
                dma(()),
                dma(()),
            ],
            compiler_params=pltpu.CompilerParams(collective_id=number, has_side_effects=True),
            name="sketch_gram",
        )(
            hidden_panel.reshape(2, ny, 2, nz, 8, length),
            row_signs.reshape(1, length),
            sample_rows,
            sample_counts.reshape(1, shards),
            ridge_weight.reshape(1, 1),
        )

    small = full * 3 // 512 * 128
    if small == 0:
        return run(full, 0).T
    result = lax.cond(jnp.sum(sample_counts) <= small, lambda: run(small, 1), lambda: run(full, 0))
    return result.T


def solution(mesh):
    placed = (P("cols", "rows"), P("rows"), P("rows", None), P(), P())
    return jax.shard_map(
        body, mesh=mesh, in_specs=placed, out_specs=P("cols", "rows"), check_vma=False
    )
```
